128 devices in a mesh: seq: 4 (over x), req: 32 (over z, y, core).
Axes of the slice: x: 4, y: 4, z: 4, core: 2. Of those that a mesh axis runs over, the one named last changes fastest.
Arguments:
- stream_tokens: bfloat16 [65536, 2048], P(('seq', 'req')), may hold values from -6 to 6
- xbc_weight: bfloat16 [2048, 5120], P(None, ('seq', 'req')), may hold values from -0.125 to 0.125
- step_weight: bfloat16 [2048, 64], replicated, may hold values from -0.125 to 0.125
- conv_weight: float32 [4, 5120], replicated, may hold values from -3 to 3
- conv_bias: float32 [5120], replicated, may hold values from -3 to 3
- step_bias: float32 [64], replicated, may hold values from -6 to -4
- decay_rate: float32 [64], replicated, may hold values from 0.02 to 3
- skip_gain: float32 [64], replicated, may hold values from 0.1 to 0.5
- norm_gain: float32 [4096], replicated, may hold values from 0.5 to 1.5
- segment_ids: int32 [32, 2048], P('req'), may hold values from 0 to 1, never falling along the last dimension, each value on 1 to 1536 neighbouring positions
- page_target: int32 [128, 32], P(('seq', 'req')), may hold values from 0 to 31, each once within a row
Outputs:
- mixer_out: bfloat16 [65536, 4096], P(('seq', 'req'))
The draws below stay inside these ranges and needn't reach their ends.
Inputs may be any that keep to these rules, and one draw needn't show every extreme that they name: `segment_ids`: along each row the ids never fall; each request holds 512 to 1536 consecutive tokens. `page_target`: each row holds every request group's index once.
All inputs are finite; a program needn't handle non-finite values.
Results may differ from the reference program's by a relative error of at most 0.0066.
Values may be sent and summed in bfloat16 or wider, within the bound.
No kernel may reach another device: no remote copies, remote signals or barrier semaphores. Data moves between devices by JAX's collectives and lax.ppermute only.
A program may use at most 128 MiB of HBM per device.

```python
import math
from functools import partial
import jax
import jax.numpy as jnp
import numpy as np
from jax import lax

D = 2048
HEADS = 64
HEAD_DIM = 64
GROUPS = 4
STATE = 128
KCONV = 4
SPAN = 256
SEGS = 2
TOK_DEV = 512
INNER = 4096
XBC = 5120
PAGE = 16
TOKENS = 65536
N_SEQ = 4
N_REQ = 32


def levels(rng, extent, cuts, smallest, high):
    def one(axis_at, blocks):
        steps = jax.random.uniform(jax.random.fold_in(jax.random.fold_in(rng, 6), axis_at), (blocks,), jnp.float32, smallest / len(cuts), high / len(cuts))
        return jnp.repeat(jnp.exp(steps), extent[axis_at] // blocks).reshape((-1,) + (1,) * (len(extent) - axis_at - 1))

    loudness = one(*cuts[0])
    for cut in cuts[1:]:
        loudness = loudness * one(*cut)
    return loudness


def profile(number_of, total, most, slope):
    loads = [(1 << 20) // math.isqrt(rank ** slope) + 1 for rank in range(2, number_of + 1)]
    rest, holding = total - most - (number_of - 1), [1] * (number_of - 1)
    while rest > 0:
        movable = [i for i in range(number_of - 1) if holding[i] < most]
        pool, budget = sum([loads[i] for i in movable]), rest
        for i in movable:
            more = min(most - holding[i], max(1, budget * loads[i] // pool), rest)
            holding[i] = holding[i] + more
            rest = rest - more
    return np.array([most] + holding)


def uneven(key, amount, total, limit, lean):
    if amount == 2:
        one = jax.random.randint(key, (), max(1, total - limit), min(limit, total - 1) + 1)
        return jnp.stack([one, total - one])
    sizes = jnp.asarray(profile(amount, total, limit, lean), jnp.int32)
    pairs = (amount - 1) // 2
    donor, taker = sizes[1:1 + 2 * pairs:2], sizes[2:2 + 2 * pairs:2]
    slack = jnp.minimum(donor - 1, limit - taker)
    moved = jax.random.randint(jax.random.fold_in(key, 1), (pairs,), 0, 1 << 20) % (slack + 1)
    sizes = sizes.at[1:1 + 2 * pairs:2].set(donor - moved).at[2:2 + 2 * pairs:2].set(taker + moved)
    return sizes[jax.random.permutation(jax.random.fold_in(key, 2), amount)]


def bell_draw(own_key, dims, scale, bound, shards=(), kind=jnp.bfloat16):
    drawn = jax.random.normal(own_key, dims, jnp.float32) * scale
    if len(shards) > 0:
        drawn = levels(own_key, dims, shards, -0.22, 0.18) * drawn
    return jnp.clip(drawn, min=-bound, max=bound).astype(kind)


def setup_inputs(seed: int = 0) -> dict:
    key_list = jax.random.split(jax.random.key(seed), 12)
    return {
        "stream_tokens": bell_draw(key_list[0], (TOKENS, D), 1.0, 6.0, ((0, 128),)),
        "xbc_weight": bell_draw(key_list[1], (D, XBC), D ** -0.5, 0.125, ((1, 128),)),
        "step_weight": bell_draw(key_list[2], (D, HEADS), D ** -0.5, 0.125),
        "conv_weight": bell_draw(key_list[3], (KCONV, XBC), KCONV ** -0.5, 3.0, (), jnp.float32),
        "conv_bias": bell_draw(key_list[4], (XBC,), 0.5, 3.0, (), jnp.float32),
        "step_bias": jnp.clip(jax.random.uniform(key_list[5], (HEADS,), jnp.float32, -6.0, -4.0), -6.0, -4.0),
        "decay_rate": jnp.clip(jnp.exp(jax.random.uniform(key_list[6], (HEADS,), jnp.float32, math.log(0.02), math.log(3.0))), 0.02, 3.0),
        "skip_gain": jnp.clip(jax.random.uniform(key_list[7], (HEADS,), jnp.float32, 0.1, 0.5), 0.1, 0.5),
        "norm_gain": jnp.clip(1.0 + 0.1 * jax.random.normal(key_list[8], (INNER,), jnp.float32), 0.5, 1.5),
        "segment_ids": jax.vmap(lambda own: jnp.searchsorted(jnp.cumsum(uneven(own, SEGS, N_SEQ * TOK_DEV, 3 * TOK_DEV, 2)), jnp.arange(N_SEQ * TOK_DEV), side="right"))(jax.random.split(key_list[9], N_REQ)).reshape((N_REQ, N_SEQ * TOK_DEV)).astype(jnp.int32),
        "page_target": jax.vmap(lambda own: jax.random.permutation(own, N_REQ))(jax.random.split(key_list[10], (N_SEQ * N_REQ))).reshape((N_SEQ * N_REQ, N_REQ)).astype(jnp.int32),
    }


def conv_rows(raw_rows, seg_rows, prev_raw, prev_seg, conv_weight, conv_bias):
    conv_taps = conv_weight.shape[0]
    row_count = raw_rows.shape[0]
    stacked = jnp.concatenate([prev_raw, raw_rows], axis=0).astype(jnp.float32)
    labels = jnp.concatenate([prev_seg, seg_rows], axis=0)
    summed = conv_bias[None, :] + conv_weight[conv_taps - 1][None, :] * stacked[conv_taps - 1:]
    for offset in range(conv_taps - 1):
        matching = (labels[offset:offset + row_count] == seg_rows).astype(jnp.float32)
        summed = summed + conv_weight[offset][None, :] * stacked[offset:offset + row_count] * matching[:, None]
    return jax.nn.silu(summed).astype(jnp.bfloat16)

def span_step(decay_rate, state, pieces):
    x_heads, b_mat, c_mat, step_size, seg_rows, seg_before = pieces
    span_len, head_count, head_dim = x_heads.shape
    group_count, state_dim = (b_mat.shape[1], b_mat.shape[2])
    per_group = head_count // group_count
    log_decay = jnp.cumsum(-step_size * decay_rate[None, :], axis=0)
    places = jnp.arange(span_len)
    allowed = (seg_rows[:, None] == seg_rows[None, :]) & (places[:, None] >= places[None, :])
    scores = jnp.einsum('tgn,ugn->gtu', c_mat.astype(jnp.float32), b_mat.astype(jnp.float32))
    spread = log_decay.T[:, :, None] - log_decay.T[:, None, :]
    decays = jnp.where(allowed[None], jnp.exp(jnp.where(allowed[None], spread, 0.0)), 0.0)
    mixing = (scores.reshape(group_count, 1, span_len, span_len) * decays.reshape(group_count, per_group, span_len, span_len) * step_size.T.reshape(group_count, per_group, 1, span_len)).astype(jnp.bfloat16)
    inside = jnp.einsum('ghtu,ughp->tghp', mixing.astype(jnp.float32), x_heads.reshape(span_len, group_count, per_group, head_dim).astype(jnp.float32))
    keeping = (seg_rows == seg_before).astype(jnp.float32)
    readout = jnp.einsum('tgn,ghpn->tghp', c_mat.astype(jnp.float32), state.reshape(group_count, per_group, head_dim, state_dim), precision=lax.Precision.HIGHEST)
    carried = readout * (keeping[:, None] * jnp.exp(log_decay)).reshape(span_len, group_count, per_group, 1)
    final_seg = seg_rows[span_len - 1]
    tail_weight = jnp.where(seg_rows[:, None] == final_seg, jnp.exp(log_decay[span_len - 1][None, :] - log_decay), 0.0) * step_size
    weighted = (x_heads.astype(jnp.float32) * tail_weight[:, :, None]).astype(jnp.bfloat16)
    gained = jnp.einsum('ughp,ugn->ghpn', weighted.reshape(span_len, group_count, per_group, head_dim).astype(jnp.float32), b_mat.astype(jnp.float32))
    passing = jnp.where(final_seg == seg_before, jnp.exp(log_decay[span_len - 1]), 0.0)
    new_state = passing[:, None, None] * state + gained.reshape(head_count, head_dim, state_dim)
    return (new_state, (inside + carried).reshape(span_len, head_count * head_dim))

def normalize(mixed_rows, x_heads, skip_gain, norm_gain):
    combined = mixed_rows + (x_heads.astype(jnp.float32) * skip_gain[None, :, None]).reshape(mixed_rows.shape)
    power = lax.optimization_barrier(jnp.mean(combined * combined, axis=-1, keepdims=True))
    return (combined * lax.rsqrt(power + 1e-05) * norm_gain[None, :]).astype(jnp.bfloat16)

def group_pass(token_rows, seg_rows, xbc_weight, step_weight, conv_weight, conv_bias, step_bias, decay_rate, skip_gain, norm_gain):
    raw_rows = jnp.dot(token_rows, xbc_weight, preferred_element_type=jnp.float32).astype(jnp.bfloat16)
    step_raw = jnp.dot(token_rows, step_weight, preferred_element_type=jnp.float32).astype(jnp.bfloat16)
    conv_out = conv_rows(raw_rows, seg_rows, jnp.zeros((KCONV - 1, XBC), jnp.bfloat16), jnp.full((KCONV - 1,), -1, jnp.int32), conv_weight, conv_bias)
    step_size = jax.nn.softplus(step_raw.astype(jnp.float32) + step_bias[None, :])
    row_count = token_rows.shape[0]
    x_heads = conv_out[:, :INNER].reshape(row_count, HEADS, HEAD_DIM)
    b_mat = conv_out[:, INNER:INNER + GROUPS * STATE].reshape(row_count, GROUPS, STATE)
    c_mat = conv_out[:, INNER + GROUPS * STATE:].reshape(row_count, GROUPS, STATE)
    blocks = row_count // SPAN
    block_ends = seg_rows.reshape(blocks, SPAN)[:, SPAN - 1]
    before = jnp.concatenate([jnp.full((1,), -1, jnp.int32), block_ends[:-1].astype(jnp.int32)])
    pieces = (x_heads.reshape(blocks, SPAN, HEADS, HEAD_DIM), b_mat.reshape(blocks, SPAN, GROUPS, STATE), c_mat.reshape(blocks, SPAN, GROUPS, STATE), step_size.reshape(blocks, SPAN, HEADS), seg_rows.reshape(blocks, SPAN), before)
    _, outputs = lax.scan(partial(span_step, decay_rate), jnp.zeros((HEADS, HEAD_DIM, STATE), jnp.float32), pieces)
    return normalize(outputs.reshape(row_count, INNER), x_heads, skip_gain, norm_gain)

def reference(stream_tokens, xbc_weight, step_weight, conv_weight, conv_bias, step_bias, decay_rate, skip_gain, norm_gain, segment_ids, page_target):
    inverse = jnp.argsort(page_target, axis=1).astype(jnp.int32)
    page_blocks = stream_tokens.reshape(N_SEQ, N_REQ, N_REQ, PAGE, D)
    picked = jnp.take_along_axis(page_blocks, inverse.reshape(N_SEQ, N_REQ, N_REQ, 1, 1), axis=2)
    layout = picked.transpose(2, 0, 1, 3, 4).reshape(N_REQ, N_SEQ * TOK_DEV, D)

    def one_group(packed):
        return group_pass(packed[0], packed[1], xbc_weight, step_weight, conv_weight, conv_bias, step_bias, decay_rate, skip_gain, norm_gain)
    mixed_rows = lax.map(one_group, (layout, segment_ids))
    grouped = mixed_rows.reshape(N_REQ, N_SEQ, N_REQ, PAGE, INNER).transpose(1, 2, 0, 3, 4)
    restored = jnp.take_along_axis(grouped, page_target.reshape(N_SEQ, N_REQ, N_REQ, 1, 1), axis=2)
    return restored.reshape(TOKENS, INNER)
```

```python
from functools import partial

import jax
import jax.numpy as jnp
import numpy as np
from jax import lax
from jax.experimental import pallas as pl
from jax.experimental.pallas import tpu as pltpu
from jax.sharding import Mesh, PartitionSpec as P

HEAD_DIM = 64
STATE = 128
KCONV = 4
SPAN = 256
INNER = 4096
XBC = 5120
D = 2048
CORES = 2
HEADS = 32
GROUPS = 2
HALF = 2048
BC = GROUPS * STATE
OWN = HALF + 2 * BC
UNIT = 8
PIECE = 5
DEVICES = 128


def unit_of(core, at):
    x_units, bc_units = HALF // UNIT, BC // UNIT
    if at < x_units:
        return x_units * core + at
    if at < x_units + bc_units:
        return INNER // UNIT + bc_units * core + (at - x_units)
    return (INNER + 2 * BC) // UNIT + bc_units * core + (at - x_units - bc_units)


def weight_moves():
    wanted = [
        [divmod(unit_of(d % 2, PIECE * (d // 2) + k), PIECE) for k in range(PIECE)]
        for d in range(DEVICES)
    ]
    edges = sorted({(source, d) for d in range(DEVICES) for source, _ in wanted[d]})
    sent = [{} for _ in range(DEVICES)]
    got = [{} for _ in range(DEVICES)]

    def free(table):
        return next(k for k in range(DEVICES) if k not in table)

    for source, d in edges:
        a, b = free(sent[source]), free(got[d])
        if a != b:
            path, at, tables, other, colour = [], d, got, sent, a
            while colour in tables[at]:
                nxt = tables[at][colour]
                path.append((nxt, at, colour) if tables is got else (at, nxt, colour))
                at, tables, other = nxt, other, tables
                colour = b if colour == a else a
            for s, t, colour in path:
                del sent[s][colour]
                del got[t][colour]
            for s, t, colour in path:
                sent[s][a + b - colour] = t
                got[t][a + b - colour] = s
        sent[source][a] = d
        got[d][a] = source
    rounds = 1 + max(k for table in got for k in table)
    pairs = [[(got[d][k], d) for d in range(DEVICES) if k in got[d]] for k in range(rounds)]
    picks = np.zeros((DEVICES, PIECE), np.int32)
    for d in range(DEVICES):
        where = {source: k for k, source in got[d].items()}
        picks[d] = [where[source] * PIECE + slot for source, slot in wanted[d]]
    return pairs, picks


ALL = ("seq", "chip", "core")
REQ = ("chip", "core")


def move(index_ref, source_ref, out_ref, sems, *, places):
    copies = []
    for k, (source, target) in enumerate(places(index_ref)):
        copies.append(
            pltpu.make_async_copy(source_ref.at[source], out_ref.at[target], sems.at[k])
        )
    for copy in copies:
        copy.start()
    for copy in copies:
        copy.wait()


def scatter_pages(pages, targets):
    count = pages.shape[0]
    return pl.pallas_call(
        partial(move, places=lambda index: [(k, index[k]) for k in range(count)]),
        out_shape=jax.ShapeDtypeStruct(pages.shape, pages.dtype),
        in_specs=[pl.BlockSpec(memory_space=pltpu.SMEM), pl.BlockSpec(memory_space=pl.ANY)],
        out_specs=pl.BlockSpec(memory_space=pl.ANY),
        scratch_shapes=[pltpu.SemaphoreType.DMA((count,))],
        name="scatter_pages",
    )(targets, pages)


def pick_units(units, picks):
    count = picks.shape[0]
    return pl.pallas_call(
        partial(move, places=lambda index: [(index[k], k) for k in range(count)]),
        out_shape=jax.ShapeDtypeStruct((count,) + units.shape[1:], units.dtype),
        in_specs=[pl.BlockSpec(memory_space=pltpu.SMEM), pl.BlockSpec(memory_space=pl.ANY)],
        out_specs=pl.BlockSpec(memory_space=pl.ANY),
        scratch_shapes=[pltpu.SemaphoreType.DMA((count,))],
        name="pick_units",
    )(picks, units)


def join_kernel(target_ref, own_ref, other_ref, out_ref, sems):
    copies = []
    for k in range(own_ref.shape[0]):
        group = target_ref[k]
        for part, (pages, page) in enumerate(((own_ref, group), (other_ref, group ^ 1))):
            half = (group & 1) ^ part
            copies.append(
                pltpu.make_async_copy(
                    pages.at[page],
                    out_ref.at[k, :, pl.ds(pl.multiple_of(half * HALF, HALF), HALF)],
                    sems.at[2 * k + part],
                )
            )
    for copy in copies:
        copy.start()
    for copy in copies:
        copy.wait()


def join_pages(own, other, targets):
    count, rows, width = own.shape
    return pl.pallas_call(
        join_kernel,
        out_shape=jax.ShapeDtypeStruct((count, rows, 2 * width), own.dtype),
        in_specs=[pl.BlockSpec(memory_space=pltpu.SMEM)] + [pl.BlockSpec(memory_space=pl.ANY)] * 2,
        out_specs=pl.BlockSpec(memory_space=pl.ANY),
        scratch_shapes=[pltpu.SemaphoreType.DMA((2 * count,))],
        name="join_pages",
    )(targets, own, other)


def conv_rows(stacked, labels, conv_weight, conv_bias):
    row_count = stacked.shape[0] - (KCONV - 1)
    stacked = stacked.astype(jnp.float32)
    seg_rows = labels[KCONV - 1 :]
    summed = conv_bias[None, :] + conv_weight[KCONV - 1][None, :] * stacked[KCONV - 1 :]
    for offset in range(KCONV - 1):
        matching = (labels[offset : offset + row_count] == seg_rows).astype(jnp.float32)
        summed = (
            summed
            + conv_weight[offset][None, :]
            * stacked[offset : offset + row_count]
            * matching[:, None]
        )
    return jax.nn.silu(summed).astype(jnp.bfloat16)


def state_readout(c_mat, state_four):
    upper = state_four.astype(jnp.bfloat16)
    lower = (state_four - upper.astype(jnp.float32)).astype(jnp.bfloat16)
    first = jnp.einsum("tgn,ghpn->tghp", c_mat, upper, preferred_element_type=jnp.float32)
    second = jnp.einsum("tgn,ghpn->tghp", c_mat, lower, preferred_element_type=jnp.float32)
    return first + second


def span_step(decay_rate, state, pieces):
    x_heads, b_mat, c_mat, step_size, seg_rows, seg_before = pieces
    span_len, head_count, head_dim = x_heads.shape
    group_count, state_dim = (b_mat.shape[1], b_mat.shape[2])
    per_group = head_count // group_count
    log_decay = jnp.cumsum(-step_size * decay_rate[None, :], axis=0)
    places = jnp.arange(span_len)
    allowed = (seg_rows[:, None] == seg_rows[None, :]) & (places[:, None] >= places[None, :])
    scores = jnp.einsum("tgn,ugn->gtu", c_mat, b_mat, preferred_element_type=jnp.float32)
    spread = log_decay.T[:, :, None] - log_decay.T[:, None, :]
    decays = jnp.where(allowed[None], jnp.exp(jnp.where(allowed[None], spread, 0.0)), 0.0)
    mixing = (
        scores.reshape(group_count, 1, span_len, span_len)
        * decays.reshape(group_count, per_group, span_len, span_len)
        * step_size.T.reshape(group_count, per_group, 1, span_len)
    ).astype(jnp.bfloat16)
    inside = jnp.einsum(
        "ghtu,ughp->tghp",
        mixing,
        x_heads.reshape(span_len, group_count, per_group, head_dim),
        preferred_element_type=jnp.float32,
    )
    keeping = (seg_rows == seg_before).astype(jnp.float32)
    readout = state_readout(c_mat, state.reshape(group_count, per_group, head_dim, state_dim))
    carried = readout * (keeping[:, None] * jnp.exp(log_decay)).reshape(
        span_len, group_count, per_group, 1
    )
    final_seg = seg_rows[span_len - 1]
    tail_weight = (
        jnp.where(
            seg_rows[:, None] == final_seg,
            jnp.exp(log_decay[span_len - 1][None, :] - log_decay),
            0.0,
        )
        * step_size
    )
    weighted = (x_heads.astype(jnp.float32) * tail_weight[:, :, None]).astype(jnp.bfloat16)
    gained = jnp.einsum(
        "ughp,ugn->ghpn",
        weighted.reshape(span_len, group_count, per_group, head_dim),
        b_mat,
        preferred_element_type=jnp.float32,
    )
    passing = jnp.where(final_seg == seg_before, jnp.exp(log_decay[span_len - 1]), 0.0)
    new_state = passing[:, None, None] * state + gained.reshape(head_count, head_dim, state_dim)
    return (new_state, (inside + carried).reshape(span_len, head_count * head_dim))


def request(tokens, halo, labels, weight, step_weight, conv_weight, conv_bias, step_bias, decay_rate, skip_gain):
    tok_rows = tokens.shape[0]
    rows = jnp.concatenate([halo[halo.shape[0] - (KCONV - 1) :], tokens], axis=0)
    raw_rows = lax.dot_general(
        rows, weight, (((1,), (1,)), ((), ())), preferred_element_type=jnp.float32
    ).astype(jnp.bfloat16)
    step_raw = jnp.dot(tokens, step_weight, preferred_element_type=jnp.float32).astype(jnp.bfloat16)
    seg_rows = labels[KCONV - 1 :]
    seg_before = labels[KCONV - 2]
    conv_out = conv_rows(raw_rows, labels, conv_weight, conv_bias)
    step_size = jax.nn.softplus(step_raw.astype(jnp.float32) + step_bias[None, :])
    x_heads = conv_out[:, :HALF].reshape(tok_rows, HEADS, HEAD_DIM)
    b_mat = conv_out[:, HALF : HALF + BC].reshape(tok_rows, GROUPS, STATE)
    c_mat = conv_out[:, HALF + BC :].reshape(tok_rows, GROUPS, STATE)
    blocks = tok_rows // SPAN
    block_ends = seg_rows.reshape(blocks, SPAN)[:, SPAN - 1]
    before = jnp.concatenate([seg_before[None], block_ends[:-1]])
    pieces = (
        x_heads.reshape(blocks, SPAN, HEADS, HEAD_DIM),
        b_mat.reshape(blocks, SPAN, GROUPS, STATE),
        c_mat.reshape(blocks, SPAN, GROUPS, STATE),
        step_size.reshape(blocks, SPAN, HEADS),
        seg_rows.reshape(blocks, SPAN),
        before,
    )
    local_state, outputs = lax.scan(
        partial(span_step, decay_rate), jnp.zeros((HEADS, HEAD_DIM, STATE), jnp.float32), pieces
    )
    log_decay = jnp.cumsum(-step_size * decay_rate[None, :], axis=0)
    through = jnp.where(seg_rows[tok_rows - 1] == seg_before, jnp.exp(log_decay[tok_rows - 1]), 0.0)
    states = lax.all_gather(local_state.astype(jnp.bfloat16), "seq")
    throughs = lax.all_gather(jnp.broadcast_to(through[None, :], (8, HEADS)), "seq")[:, 0]
    here = lax.axis_index("seq")
    incoming = jnp.zeros((HEADS, HEAD_DIM, STATE), jnp.float32)
    for at in range(lax.axis_size("seq") - 1):
        after = throughs[at][:, None, None] * incoming + states[at].astype(jnp.float32)
        incoming = jnp.where(at < here, after, incoming)
    readout = state_readout(c_mat, incoming.reshape(GROUPS, HEADS // GROUPS, HEAD_DIM, STATE))
    keeping = (seg_rows == seg_before).astype(jnp.float32)
    factor = keeping[:, None] * jnp.exp(log_decay)
    mixed_rows = outputs.reshape(tok_rows, HALF) + (
        readout * factor.reshape(tok_rows, GROUPS, HEADS // GROUPS, 1)
    ).reshape(tok_rows, HALF)
    combined = mixed_rows + (x_heads.astype(jnp.float32) * skip_gain[None, :, None]).reshape(
        mixed_rows.shape
    )
    return combined, jnp.sum(combined * combined, axis=-1)


def per_device(
    stream_tokens,
    xbc_weight,
    step_weight,
    conv_weight,
    conv_bias,
    step_bias,
    decay_rate,
    skip_gain,
    norm_gain,
    segment_ids,
    page_target,
):
    groups_of_requests = lax.axis_size("chip") * CORES
    tok_rows = stream_tokens.shape[0]
    page_rows = tok_rows // groups_of_requests
    seq_at, core = lax.axis_index("seq"), lax.axis_index("core")
    flat = (seq_at * lax.axis_size("chip") + lax.axis_index("chip")) * CORES + core
    swap = [(0, 1), (1, 0)]
    peers = lax.axis_size("seq")
    onward = [(i, i + 1) for i in range(peers - 1)]
    onward_swap = [(2 * i + k, 2 * (i + 1) + 1 - k) for i in range(peers - 1) for k in range(2)]

    targets = page_target[0]
    pages = scatter_pages(stream_tokens.reshape(groups_of_requests, page_rows, D), targets)
    own = lax.all_to_all(pages, REQ, split_axis=0, concat_axis=0, tiled=True)
    other = lax.ppermute(own, "core", swap)
    last_page = own[groups_of_requests - 1]
    own_halo = lax.ppermute(last_page, "seq", onward)
    other_halo = lax.ppermute(last_page, ("seq", "core"), onward_swap)
    other_ids = lax.ppermute(segment_ids, "core", swap)

    pairs, picks = weight_moves()
    piece = xbc_weight.T.reshape(PIECE, UNIT, D)
    arrived = jnp.concatenate([lax.ppermute(piece, ALL, moves) for moves in pairs], axis=0)
    units = pick_units(arrived, jnp.asarray(picks)[flat])
    weight = lax.all_gather(units.reshape(PIECE * UNIT, D), ("seq", "chip"), axis=0, tiled=True)

    def columns(values):
        return jnp.concatenate(
            [
                lax.dynamic_slice_in_dim(values, core * HALF, HALF, axis=-1),
                lax.dynamic_slice_in_dim(values, INNER + core * BC, BC, axis=-1),
                lax.dynamic_slice_in_dim(values, INNER + 2 * BC + core * BC, BC, axis=-1),
            ],
            axis=-1,
        )

    def heads(values):
        return lax.dynamic_slice_in_dim(values, core * HEADS, HEADS, axis=-1)

    def labels(ids):
        padded = jnp.concatenate([jnp.full((KCONV - 1,), -1, jnp.int32), ids[0]])
        return lax.dynamic_slice_in_dim(padded, seq_at * tok_rows, tok_rows + KCONV - 1)

    shared = (
        weight,
        heads(step_weight),
        columns(conv_weight),
        columns(conv_bias),
        heads(step_bias),
        heads(decay_rate),
        heads(skip_gain),
    )
    gain = lax.dynamic_slice_in_dim(norm_gain, core * HALF, HALF)
    own_rows, own_power = request(own.reshape(tok_rows, D), own_halo, labels(segment_ids), *shared)
    other_rows, other_power = request(
        other.reshape(tok_rows, D), other_halo, labels(other_ids), *shared
    )
    swapped = lax.ppermute(jnp.stack([own_power, other_power]), "core", swap)

    def sent_back(rows, power):
        mean = power / INNER
        normed = (rows * lax.rsqrt(mean[:, None] + 1e-05) * gain[None, :]).astype(jnp.bfloat16)
        return lax.all_to_all(
            normed.reshape(groups_of_requests, page_rows, HALF),
            REQ,
            split_axis=0,
            concat_axis=0,
            tiled=True,
        )

    own_back = sent_back(own_rows, own_power + swapped[1])
    other_back = sent_back(other_rows, other_power + swapped[0])
    return join_pages(own_back, other_back, targets).reshape(tok_rows, INNER)


def solution(mesh):
    chips = mesh.shape["req"] // CORES
    by_core = Mesh(
        mesh.devices.reshape(mesh.shape["seq"], chips, CORES), ("seq", "chip", "core")
    )
    in_specs = (
        P(ALL, None),
        P(None, ALL),
        P(),
        P(),
        P(),
        P(),
        P(),
        P(),
        P(),
        P(REQ, None),
        P(ALL, None),
    )
    return jax.shard_map(
        per_device, mesh=by_core, in_specs=in_specs, out_specs=P(ALL, None), check_vma=False
    )
```

```python
from functools import partial

import jax
import jax.numpy as jnp
import numpy as np
from jax import lax
from jax.experimental import pallas as pl
from jax.experimental.pallas import tpu as pltpu
from jax.sharding import Mesh, PartitionSpec as P

HEAD_DIM = 64
STATE = 128
KCONV = 4
SPAN = 256
INNER = 4096
XBC = 5120
D = 2048
CORES = 2
HEADS = 32
GROUPS = 2
HALF = 2048
BC = GROUPS * STATE
OWN = HALF + 2 * BC
UNIT = 8
PIECE = 5
DEVICES = 128


def unit_of(core, at):
    x_units, bc_units = HALF // UNIT, BC // UNIT
    if at < x_units:
        return x_units * core + at
    if at < x_units + bc_units:
        return INNER // UNIT + bc_units * core + (at - x_units)
    return (INNER + 2 * BC) // UNIT + bc_units * core + (at - x_units - bc_units)


def weight_moves():
    wanted = [
        [divmod(unit_of(d % 2, PIECE * (d // 2) + k), PIECE) for k in range(PIECE)]
        for d in range(DEVICES)
    ]
    edges = sorted({(source, d) for d in range(DEVICES) for source, _ in wanted[d]})
    sent = [{} for _ in range(DEVICES)]
    got = [{} for _ in range(DEVICES)]

    def free(table):
        return next(k for k in range(DEVICES) if k not in table)

    for source, d in edges:
        a, b = free(sent[source]), free(got[d])
        if a != b:
            path, at, tables, other, colour = [], d, got, sent, a
            while colour in tables[at]:
                nxt = tables[at][colour]
                path.append((nxt, at, colour) if tables is got else (at, nxt, colour))
                at, tables, other = nxt, other, tables
                colour = b if colour == a else a
            for s, t, colour in path:
                del sent[s][colour]
                del got[t][colour]
            for s, t, colour in path:
                sent[s][a + b - colour] = t
                got[t][a + b - colour] = s
        sent[source][a] = d
        got[d][a] = source
    rounds = 1 + max(k for table in got for k in table)
    pairs = [[(got[d][k], d) for d in range(DEVICES) if k in got[d]] for k in range(rounds)]
    picks = np.zeros((DEVICES, PIECE), np.int32)
    for d in range(DEVICES):
        where = {source: k for k, source in got[d].items()}
        picks[d] = [where[source] * PIECE + slot for source, slot in wanted[d]]
    return pairs, picks


ALL = ("seq", "chip", "core")
REQ = ("chip", "core")


def move(index_ref, source_ref, out_ref, sems, *, places):
    copies = []
    for k, (source, target) in enumerate(places(index_ref)):
        copies.append(
            pltpu.make_async_copy(source_ref.at[source], out_ref.at[target], sems.at[k])
        )
    for copy in copies:
        copy.start()
    for copy in copies:
        copy.wait()


def scatter_pages(pages, targets):
    count = pages.shape[0]
    return pl.pallas_call(
        partial(move, places=lambda index: [(k, index[k]) for k in range(count)]),
        out_shape=jax.ShapeDtypeStruct(pages.shape, pages.dtype),
        in_specs=[pl.BlockSpec(memory_space=pltpu.SMEM), pl.BlockSpec(memory_space=pl.ANY)],
        out_specs=pl.BlockSpec(memory_space=pltpu.VMEM),
        scratch_shapes=[pltpu.SemaphoreType.DMA((count,))],
        name="scatter_pages",
    )(targets, pages)


def pick_units(units, picks):
    count = picks.shape[0]
    return pl.pallas_call(
        partial(move, places=lambda index: [(index[k], k) for k in range(count)]),
        out_shape=jax.ShapeDtypeStruct((count,) + units.shape[1:], units.dtype),
        in_specs=[pl.BlockSpec(memory_space=pltpu.SMEM), pl.BlockSpec(memory_space=pl.ANY)],
        out_specs=pl.BlockSpec(memory_space=pltpu.VMEM),
        scratch_shapes=[pltpu.SemaphoreType.DMA((count,))],
        name="pick_units",
    )(picks, units)


def join_kernel(target_ref, own_ref, other_ref, out_ref, sems):
    copies = []
    for k in range(own_ref.shape[0]):
        group = target_ref[k]
        for part, (pages, page) in enumerate(((own_ref, group), (other_ref, group ^ 1))):
            half = (group & 1) ^ part
            copies.append(
                pltpu.make_async_copy(
                    pages.at[page],
                    out_ref.at[k, :, pl.ds(pl.multiple_of(half * HALF, HALF), HALF)],
                    sems.at[2 * k + part],
                )
            )
    for copy in copies:
        copy.start()
    for copy in copies:
        copy.wait()


def join_pages(own, other, targets):
    count, rows, width = own.shape
    return pl.pallas_call(
        join_kernel,
        out_shape=jax.ShapeDtypeStruct((count, rows, 2 * width), own.dtype),
        in_specs=[pl.BlockSpec(memory_space=pltpu.SMEM)] + [pl.BlockSpec(memory_space=pl.ANY)] * 2,
        out_specs=pl.BlockSpec(memory_space=pltpu.VMEM),
        scratch_shapes=[pltpu.SemaphoreType.DMA((2 * count,))],
        name="join_pages",
    )(targets, own, other)


INTERPRET = False
LOG2E = 1.4426950408889634
ROWS = 512
BLOCKS = ROWS // SPAN
CONV_COLS = 512
CHUNK = 256
HALO = 16
TERMS = 3
SENT = STATE + 16
HEADS_STEP = 4
STEP_COLS = HEADS_STEP * HEAD_DIM
PER_GROUP = HEADS // GROUPS
GROUP_COLS = PER_GROUP * HEAD_DIM


def conv_kernel(halo_ref, tok_ref, weight_ref, taps_ref, bias_ref, mask_ref, out_ref, raw_ref):
    masks = [mask_ref[:, k : k + 1] for k in range(KCONV - 1)]
    for part in range(CONV_COLS // CHUNK):
        cols = slice(part * CHUNK, (part + 1) * CHUNK)
        weight = weight_ref[cols, :]
        dims = (((1,), (1,)), ((), ()))
        raw_ref[part, :HALO, :] = (
            lax.dot_general(halo_ref[...], weight, dims, preferred_element_type=jnp.float32)
            .astype(jnp.bfloat16)
            .astype(jnp.float32)
        )
        raw_ref[part, HALO:, :] = (
            lax.dot_general(tok_ref[...], weight, dims, preferred_element_type=jnp.float32)
            .astype(jnp.bfloat16)
            .astype(jnp.float32)
        )
    for part in range(CONV_COLS // CHUNK):
        cols = slice(part * CHUNK, (part + 1) * CHUNK)
        summed = bias_ref[:, cols] + taps_ref[KCONV - 1 : KCONV, cols] * raw_ref[part, HALO:, :]
        for k in range(KCONV - 1):
            start = HALO - (KCONV - 1) + k
            summed = (
                summed
                + (taps_ref[k : k + 1, cols] * raw_ref[part, start : start + ROWS, :]) * masks[k]
            )
        out_ref[:, cols] = (summed * (0.5 + 0.5 * jnp.tanh(0.5 * summed))).astype(jnp.bfloat16)


def project_conv(halo, tokens, weight, taps, bias, masks):
    return pl.pallas_call(
        conv_kernel,
        grid=(OWN // CONV_COLS,),
        out_shape=jax.ShapeDtypeStruct((ROWS, OWN), jnp.bfloat16),
        in_specs=[
            pl.BlockSpec((HALO, D), lambda n: (0, 0)),
            pl.BlockSpec((ROWS, D), lambda n: (0, 0)),
            pl.BlockSpec((CONV_COLS, D), lambda n: (n, 0)),
            pl.BlockSpec((KCONV, CONV_COLS), lambda n: (0, n)),
            pl.BlockSpec((1, CONV_COLS), lambda n: (0, n)),
            pl.BlockSpec((ROWS, KCONV - 1), lambda n: (0, 0)),
        ],
        out_specs=pl.BlockSpec((ROWS, CONV_COLS), lambda n: (0, n)),
        scratch_shapes=[pltpu.VMEM((CONV_COLS // CHUNK, HALO + ROWS, CHUNK), jnp.float32)],
        cost_estimate=pl.CostEstimate(
            flops=2 * (ROWS + HALO) * D * OWN, transcendentals=ROWS * OWN, bytes_accessed=15 << 20
        ),
        name="project_conv",
        interpret=INTERPRET,
    )(halo, tokens, weight, taps, bias, masks)


def spread_heads(values, first_head, columns):
    upper = values.astype(jnp.bfloat16)
    lower = (values - upper.astype(jnp.float32)).astype(jnp.bfloat16)
    head = lax.broadcasted_iota(jnp.int32, (HEADS, columns), 0)
    column = lax.broadcasted_iota(jnp.int32, (HEADS, columns), 1)
    chosen = (head == first_head + column // HEAD_DIM).astype(jnp.bfloat16)
    return jnp.dot(upper, chosen, preferred_element_type=jnp.float32) + jnp.dot(
        lower, chosen, preferred_element_type=jnp.float32
    )


def state_kernel(x_ref, b_ref, tail_ref, row_ref, gained_ref, local_ref):
    tail = spread_heads(tail_ref[...], pl.program_id(0) * PER_GROUP, GROUP_COLS)
    weighted = (x_ref[...].astype(jnp.float32) * tail).astype(jnp.bfloat16)
    gained = [
        lax.dot_general(
            b_ref[b * SPAN : (b + 1) * SPAN, :],
            weighted[b * SPAN : (b + 1) * SPAN],
            (((0,), (0,)), ((), ())),
            preferred_element_type=jnp.float32,
        )
        for b in range(BLOCKS)
    ]
    gained_ref[...] = gained[0]
    local_ref[:STATE, :] = (row_ref[1:2, :] * gained[0] + gained[1]).astype(jnp.bfloat16)
    left = row_ref[0:1, :] * row_ref[1:2, :]
    row = lax.broadcasted_iota(jnp.int32, (SENT - STATE, GROUP_COLS), 0)
    terms = jnp.zeros((SENT - STATE, GROUP_COLS), jnp.float32)
    for at in range(TERMS):
        term = left.astype(jnp.bfloat16).astype(jnp.float32)
        terms = jnp.where(row == at, term, terms)
        left = left - term
    local_ref[STATE:, :] = terms.astype(jnp.bfloat16)


def block_states(conv_out, tail, rows):
    return pl.pallas_call(
        state_kernel,
        grid=(GROUPS,),
        out_shape=[
            jax.ShapeDtypeStruct((STATE, HALF), jnp.float32),
            jax.ShapeDtypeStruct((SENT, HALF), jnp.bfloat16),
        ],
        in_specs=[
            pl.BlockSpec((ROWS, GROUP_COLS), lambda g: (0, g)),
            pl.BlockSpec((ROWS, STATE), lambda g: (0, HALF // STATE + g)),
            pl.BlockSpec((ROWS, HEADS), lambda g: (0, 0)),
            pl.BlockSpec((8, GROUP_COLS), lambda g: (0, g)),
        ],
        out_specs=[
            pl.BlockSpec((STATE, GROUP_COLS), lambda g: (0, g)),
            pl.BlockSpec((SENT, GROUP_COLS), lambda g: (0, g)),
        ],
        cost_estimate=pl.CostEstimate(
            flops=2 * ROWS * HALF * STATE, transcendentals=0, bytes_accessed=4 << 20
        ),
        name="block_states",
        interpret=INTERPRET,
    )(conv_out, conv_out, tail, rows)


def mixing_kernel(x_ref, b_ref, c_ref, decay_ref, seg_ref, out_ref, scores_ref, bias_ref):
    @pl.when(pl.program_id(1) == 0)
    def _():
        at = lax.broadcasted_iota(jnp.int32, (SPAN, SPAN), 0)
        source = lax.broadcasted_iota(jnp.int32, (SPAN, SPAN), 1)
        for b in range(BLOCKS):
            rows = slice(b * SPAN, (b + 1) * SPAN)
            scores_ref[b] = lax.dot_general(
                c_ref[rows, :],
                b_ref[rows, :],
                (((1,), (1,)), ((), ())),
                preferred_element_type=jnp.float32,
            )
            across = seg_ref[:, rows]
            down = across.T[:, 0:1]
            allowed = (down == across[0:1, :]) & (at >= source)
            bias_ref[b] = jnp.where(allowed, 0.0, -1e30)

    half = SPAN // 2
    lane = lax.broadcasted_iota(jnp.int32, (half, 2 * HEAD_DIM), 1)
    for b in range(BLOCKS):
        decay = decay_ref[0, :, b * SPAN : (b + 1) * SPAN]
        down = decay.T
        for pair in range(HEADS_STEP // 2):
            cols = slice(pair * 2 * HEAD_DIM, (pair + 1) * 2 * HEAD_DIM)
            for part in range(2):
                reach = (part + 1) * half
                rows = slice(part * half, reach)
                found = []
                for head in (2 * pair, 2 * pair + 1):
                    spread = (
                        down[rows, head : head + 1]
                        - decay[HEADS_STEP + head : HEADS_STEP + head + 1, :reach]
                    )
                    mixing = (
                        jnp.exp2(spread + bias_ref[b, rows, :reach]) * scores_ref[b, rows, :reach]
                    ).astype(jnp.bfloat16)
                    found.append(
                        jnp.dot(
                            mixing,
                            x_ref[b * SPAN : b * SPAN + reach, cols],
                            preferred_element_type=jnp.float32,
                        )
                    )
                out_ref[b * SPAN + part * half : b * SPAN + reach, cols] = jnp.where(
                    lane < HEAD_DIM, found[0], found[1]
                )


def mix_blocks(conv_out, decay, seg):
    steps = PER_GROUP // HEADS_STEP
    return pl.pallas_call(
        mixing_kernel,
        grid=(GROUPS, steps),
        out_shape=jax.ShapeDtypeStruct((ROWS, HALF), jnp.float32),
        in_specs=[
            pl.BlockSpec((ROWS, STEP_COLS), lambda g, p: (0, g * steps + p)),
            pl.BlockSpec((ROWS, STATE), lambda g, p: (0, HALF // STATE + g)),
            pl.BlockSpec((ROWS, STATE), lambda g, p: (0, HALF // STATE + GROUPS + g)),
            pl.BlockSpec((1, 8, ROWS), lambda g, p: (g * steps + p, 0, 0)),
            pl.BlockSpec((8, ROWS), lambda g, p: (0, 0)),
        ],
        out_specs=pl.BlockSpec((ROWS, STEP_COLS), lambda g, p: (0, g * steps + p)),
        scratch_shapes=[pltpu.VMEM((BLOCKS, SPAN, SPAN), jnp.float32)] * 2,
        cost_estimate=pl.CostEstimate(
            flops=2 * ROWS * SPAN * HALF,
            transcendentals=ROWS * SPAN * HEADS,
            bytes_accessed=7 << 20,
        ),
        name="mix_blocks",
        interpret=INTERPRET,
    )(conv_out, conv_out, conv_out, decay, seg)


def readout_kernel(
    y_ref, x_ref, c_ref, gained_ref, states_ref, factor_ref, row_ref, out_ref, power_ref, part_ref
):
    steps = PER_GROUP // HEADS_STEP
    at = pl.program_id(0) * steps + pl.program_id(1)
    incoming = jnp.zeros((STATE, STEP_COLS), jnp.float32)
    for peer in range(states_ref.shape[0] - 1):
        terms = states_ref[peer, STATE:, :].astype(jnp.float32)
        through = (terms[0:1] + terms[1:2]) + terms[2:3]
        after = through * incoming + states_ref[peer, :STATE, :].astype(jnp.float32)
        incoming = jnp.where(row_ref[4 + peer : 5 + peer, :] > 0.5, after, incoming)
    second = row_ref[0:1, :] * incoming + gained_ref[...]
    factor = spread_heads(factor_ref[...], at * HEADS_STEP, STEP_COLS)

    @pl.when(at == 0)
    def _():
        part_ref[...] = jnp.zeros_like(part_ref)

    for b, state in enumerate((incoming, second)):
        rows = slice(b * SPAN, (b + 1) * SPAN)
        readout = jnp.dot(
            c_ref[rows, :], state.astype(jnp.bfloat16), preferred_element_type=jnp.float32
        )
        combined = (
            y_ref[rows, :]
            + readout * factor[rows]
            + row_ref[2:3, :] * x_ref[rows, :].astype(jnp.float32)
        )
        out_ref[rows, :] = combined
        squared = combined * combined
        part_ref[rows, :] += squared[:, :128] + squared[:, 128:]

    @pl.when(at == GROUPS * steps - 1)
    def _():
        power_ref[...] = jnp.sum(part_ref[...].T, axis=0, keepdims=True)


def read_states(mixed, conv_out, gained, states, factor, rows):
    steps = PER_GROUP // HEADS_STEP
    peers = states.shape[0]
    return pl.pallas_call(
        readout_kernel,
        grid=(GROUPS, steps),
        out_shape=[
            jax.ShapeDtypeStruct((ROWS, HALF), jnp.float32),
            jax.ShapeDtypeStruct((1, ROWS), jnp.float32),
        ],
        in_specs=[
            pl.BlockSpec((ROWS, STEP_COLS), lambda g, p: (0, g * steps + p)),
            pl.BlockSpec((ROWS, STEP_COLS), lambda g, p: (0, g * steps + p)),
            pl.BlockSpec((ROWS, STATE), lambda g, p: (0, HALF // STATE + GROUPS + g)),
            pl.BlockSpec((STATE, STEP_COLS), lambda g, p: (0, g * steps + p)),
            pl.BlockSpec((peers, SENT, STEP_COLS), lambda g, p: (0, 0, g * steps + p)),
            pl.BlockSpec((ROWS, HEADS), lambda g, p: (0, 0)),
            pl.BlockSpec((8, STEP_COLS), lambda g, p: (0, g * steps + p)),
        ],
        out_specs=[
            pl.BlockSpec((ROWS, STEP_COLS), lambda g, p: (0, g * steps + p)),
            pl.BlockSpec((1, ROWS), lambda g, p: (0, 0)),
        ],
        scratch_shapes=[pltpu.VMEM((ROWS, 128), jnp.float32)],
        cost_estimate=pl.CostEstimate(
            flops=2 * ROWS * STATE * HALF, transcendentals=0, bytes_accessed=14 << 20
        ),
        name="read_states",
        interpret=INTERPRET,
    )(mixed, conv_out, conv_out, gained, states, factor, rows)


def prepare(tokens, labels, step_weight, step_bias, decay_rate):
    step_raw = jnp.dot(tokens, step_weight, preferred_element_type=jnp.float32).astype(jnp.bfloat16)
    step_size = jax.nn.softplus(step_raw.astype(jnp.float32) + step_bias[None, :])
    seg = labels[KCONV - 1 :]
    change = (-step_size * decay_rate[None, :]).reshape(BLOCKS, SPAN, HEADS)
    log_decay = jnp.cumsum(change, axis=1)
    last = log_decay[:, SPAN - 1]
    seg_blocks = seg.reshape(BLOCKS, SPAN)
    final = seg_blocks[:, SPAN - 1]
    before = jnp.concatenate([labels[KCONV - 2][None], final[:-1]])
    tail = jnp.where(
        (seg_blocks == final[:, None])[:, :, None], jnp.exp(last[:, None] - log_decay), 0.0
    ) * step_size.reshape(BLOCKS, SPAN, HEADS)
    factor = jnp.where((seg_blocks == before[:, None])[:, :, None], jnp.exp(log_decay), 0.0)
    passing = jnp.where((final == before)[:, None], jnp.exp(last), 0.0)
    masks = jnp.stack(
        [(labels[k : k + ROWS] == seg).astype(jnp.float32) for k in range(KCONV - 1)], axis=1
    )
    scaled = (log_decay * LOG2E).reshape(ROWS, HEADS).T
    sized = scaled - jnp.log2(step_size).T
    decay = jnp.concatenate(
        [
            scaled.reshape(HEADS // HEADS_STEP, HEADS_STEP, ROWS),
            sized.reshape(HEADS // HEADS_STEP, HEADS_STEP, ROWS),
        ],
        axis=1,
    )
    seg_rows = jnp.broadcast_to(seg.astype(jnp.float32)[None, :], (8, ROWS))
    return dict(
        tail=tail.reshape(ROWS, HEADS),
        factor=factor.reshape(ROWS, HEADS),
        passing=passing,
        masks=masks,
        decay=decay,
        seg=seg_rows,
    )


def over_columns(values):
    return jnp.repeat(values, HEAD_DIM, axis=-1)


def per_device(
    stream_tokens,
    xbc_weight,
    step_weight,
    conv_weight,
    conv_bias,
    step_bias,
    decay_rate,
    skip_gain,
    norm_gain,
    segment_ids,
    page_target,
):
    request_groups = lax.axis_size("chip") * CORES
    tok_rows = stream_tokens.shape[0]
    page_rows = tok_rows // request_groups
    seq_at, core = lax.axis_index("seq"), lax.axis_index("core")
    flat = (seq_at * lax.axis_size("chip") + lax.axis_index("chip")) * CORES + core
    swap = [(0, 1), (1, 0)]
    peers = lax.axis_size("seq")
    onward = [(i, i + 1) for i in range(peers - 1)]
    onward_swap = [(2 * i + k, 2 * (i + 1) + 1 - k) for i in range(peers - 1) for k in range(2)]

    targets = page_target[0]
    pages = scatter_pages(stream_tokens.reshape(request_groups, page_rows, D), targets)
    own = lax.all_to_all(pages, REQ, split_axis=0, concat_axis=0, tiled=True)
    other = lax.ppermute(own, "core", swap)
    last_page = own[request_groups - 1]
    own_halo = lax.ppermute(last_page, "seq", onward)
    other_halo = lax.ppermute(last_page, ("seq", "core"), onward_swap)
    other_ids = lax.ppermute(segment_ids, "core", swap)

    pairs, picks = weight_moves()
    piece = xbc_weight.T.reshape(PIECE, UNIT, D)
    arrived = jnp.concatenate([lax.ppermute(piece, ALL, moves) for moves in pairs], axis=0)
    units = pick_units(arrived, jnp.asarray(picks)[flat])
    weight = lax.all_gather(units.reshape(PIECE * UNIT, D), ("seq", "chip"), axis=0, tiled=True)

    def columns(values):
        return jnp.concatenate(
            [
                lax.dynamic_slice_in_dim(values, core * HALF, HALF, axis=-1),
                lax.dynamic_slice_in_dim(values, INNER + core * BC, BC, axis=-1),
                lax.dynamic_slice_in_dim(values, INNER + 2 * BC + core * BC, BC, axis=-1),
            ],
            axis=-1,
        )

    def heads(values):
        return lax.dynamic_slice_in_dim(values, core * HEADS, HEADS, axis=-1)

    def labels(ids):
        padded = jnp.concatenate([jnp.full((KCONV - 1,), -1, jnp.int32), ids[0]])
        return lax.dynamic_slice_in_dim(padded, seq_at * tok_rows, tok_rows + KCONV - 1)

    taps, bias = columns(conv_weight), columns(conv_bias[None, :])
    step_half, step_shift, rate = heads(step_weight), heads(step_bias), heads(decay_rate)
    gain = lax.dynamic_slice_in_dim(norm_gain, core * HALF, HALF)
    ahead = (jnp.arange(peers) < seq_at).astype(jnp.float32)
    fixed_rows = jnp.concatenate(
        [
            over_columns(heads(skip_gain)[None, :]),
            jnp.zeros((1, HALF), jnp.float32),
            jnp.broadcast_to(ahead[:, None], (peers, HALF)),
        ],
        axis=0,
    )

    def states(tokens, halo, ids):
        tokens = tokens.reshape(tok_rows, D)
        ready = prepare(tokens, labels(ids), step_half, step_shift, rate)
        rows = jnp.concatenate([over_columns(ready["passing"]), fixed_rows], axis=0)
        conv_out = project_conv(halo, tokens, weight, taps, bias, ready["masks"])
        gained, local = block_states(conv_out, ready["tail"], rows)
        every = lax.all_gather(local, "seq")
        return ready, rows, conv_out, gained, every

    def outputs(ready, rows, conv_out, gained, every):
        mixed = mix_blocks(conv_out, ready["decay"], ready["seg"])
        combined, power = read_states(mixed, conv_out, gained, every, ready["factor"], rows)
        return combined, power, lax.ppermute(power, "core", swap)

    def sent_back(combined, power):
        scale = lax.rsqrt(power[0] / INNER + 1e-05)
        normed = (combined * scale[:, None] * gain[None, :]).astype(jnp.bfloat16)
        return lax.all_to_all(
            normed.reshape(request_groups, page_rows, HALF),
            REQ,
            split_axis=0,
            concat_axis=0,
            tiled=True,
        )

    own_states = states(own, own_halo, segment_ids)
    other_states = states(other, other_halo, other_ids)
    own_rows, own_power, own_swapped = outputs(*own_states)
    other_rows, other_power, other_swapped = outputs(*other_states)
    own_back = sent_back(own_rows, own_power + other_swapped)
    other_back = sent_back(other_rows, other_power + own_swapped)
    return join_pages(own_back, other_back, targets).reshape(tok_rows, INNER)


def solution(mesh):
    chips = mesh.shape["req"] // CORES
    by_core = Mesh(
        mesh.devices.reshape(mesh.shape["seq"], chips, CORES), ("seq", "chip", "core")
    )
    in_specs = (
        P(ALL, None),
        P(None, ALL),
        P(),
        P(),
        P(),
        P(),
        P(),
        P(),
        P(),
        P(REQ, None),
        P(ALL, None),
    )
    return jax.shard_map(
        per_device, mesh=by_core, in_specs=in_specs, out_specs=P(ALL, None), check_vma=False
    )
```

```python
from functools import partial

import jax
import jax.numpy as jnp
import numpy as np
from jax import lax
from jax.experimental import pallas as pl
from jax.experimental.pallas import tpu as pltpu
from jax.sharding import Mesh, PartitionSpec as P

HEAD_DIM = 64
STATE = 128
KCONV = 4
SPAN = 256
INNER = 4096
XBC = 5120
D = 2048
CORES = 2
HEADS = 32
GROUPS = 2
HALF = 2048
BC = GROUPS * STATE
OWN = HALF + 2 * BC
UNIT = 8
PIECE = 5
DEVICES = 128
RANKS = DEVICES // CORES
PARTS = (HALF // GROUPS + 2 * BC, HALF // GROUPS)


def unit_of(core, at):
    first, bc_units = HALF // GROUPS // UNIT, BC // UNIT
    if at < first:
        return HALF // UNIT * core + at
    if at < first + bc_units:
        return INNER // UNIT + bc_units * core + (at - first)
    if at < first + 2 * bc_units:
        return (INNER + BC * CORES) // UNIT + bc_units * core + (at - first - bc_units)
    return HALF // UNIT * core + at - 2 * bc_units


def places_of(rank):
    early, late = PARTS[0] // UNIT // RANKS, PARTS[1] // UNIT // RANKS
    return [early * rank + k for k in range(early)] + [
        PARTS[0] // UNIT + late * rank + k for k in range(late)
    ]


def weight_moves():
    wanted = [
        [divmod(unit_of(d % CORES, at), PIECE) for at in places_of(d // CORES)]
        for d in range(DEVICES)
    ]
    edges = sorted({(source, d) for d in range(DEVICES) for source, _ in wanted[d]})
    sent = [{} for _ in range(DEVICES)]
    got = [{} for _ in range(DEVICES)]

    def free(table):
        return next(k for k in range(DEVICES) if k not in table)

    for source, d in edges:
        a, b = free(sent[source]), free(got[d])
        if a != b:
            path, at, tables, other, colour = [], d, got, sent, a
            while colour in tables[at]:
                nxt = tables[at][colour]
                path.append((nxt, at, colour) if tables is got else (at, nxt, colour))
                at, tables, other = nxt, other, tables
                colour = b if colour == a else a
            for s, t, colour in path:
                del sent[s][colour]
                del got[t][colour]
            for s, t, colour in path:
                sent[s][a + b - colour] = t
                got[t][a + b - colour] = s
        sent[source][a] = d
        got[d][a] = source
    rounds = 1 + max(k for table in got for k in table)
    pairs = [[(got[d][k], d) for d in range(DEVICES) if k in got[d]] for k in range(rounds)]
    picks = np.zeros((DEVICES, PIECE), np.int32)
    for d in range(DEVICES):
        where = {source: k for k, source in got[d].items()}
        picks[d] = [where[source] * PIECE + slot for source, slot in wanted[d]]
    return pairs, picks


ALL = ("seq", "chip", "core")
REQ = ("chip", "core")


def move(index_ref, source_ref, out_ref, sems, *, places):
    copies = []
    for k, (source, target) in enumerate(places(index_ref)):
        copies.append(
            pltpu.make_async_copy(source_ref.at[source], out_ref.at[target], sems.at[k])
        )
    for copy in copies:
        copy.start()
    for copy in copies:
        copy.wait()


def scatter_pages(pages, targets):
    count = pages.shape[0]
    return pl.pallas_call(
        partial(move, places=lambda index: [(k, index[k]) for k in range(count)]),
        out_shape=jax.ShapeDtypeStruct(pages.shape, pages.dtype),
        in_specs=[pl.BlockSpec(memory_space=pltpu.SMEM), pl.BlockSpec(memory_space=pl.ANY)],
        out_specs=pl.BlockSpec(memory_space=pltpu.VMEM),
        scratch_shapes=[pltpu.SemaphoreType.DMA((count,))],
        name="scatter_pages",
    )(targets, pages)


def pick_units(units, picks):
    count = picks.shape[0]
    return pl.pallas_call(
        partial(move, places=lambda index: [(index[k], k) for k in range(count)]),
        out_shape=jax.ShapeDtypeStruct((count,) + units.shape[1:], units.dtype),
        in_specs=[pl.BlockSpec(memory_space=pltpu.SMEM), pl.BlockSpec(memory_space=pl.ANY)],
        out_specs=pl.BlockSpec(memory_space=pltpu.VMEM),
        scratch_shapes=[pltpu.SemaphoreType.DMA((count,))],
        name="pick_units",
    )(picks, units)


def join_kernel(target_ref, even_ref, odd_ref, out_ref, sems):
    count = even_ref.shape[0]

    def copy(pages, page, k, half):
        return pltpu.make_async_copy(
            pages.at[page], out_ref.at[k, :, pl.ds(half * HALF, HALF)], sems.at[CORES * k + half]
        )

    for k in range(count):
        group = target_ref[k]
        odd = group % CORES
        for which, pages in enumerate((even_ref, odd_ref)):

            @pl.when(odd == which)
            def _():
                for half in range(CORES):
                    copy(pages, group - odd + half, k, half).start()

    for k in range(count):
        for half in range(CORES):
            copy(even_ref, 0, k, half).wait()


def join_pages(even, odd, targets):
    count, rows, width = even.shape
    return pl.pallas_call(
        join_kernel,
        out_shape=jax.ShapeDtypeStruct((count, rows, 2 * width), even.dtype),
        in_specs=[pl.BlockSpec(memory_space=pltpu.SMEM)] + [pl.BlockSpec(memory_space=pl.ANY)] * 2,
        out_specs=pl.BlockSpec(memory_space=pltpu.VMEM),
        scratch_shapes=[pltpu.SemaphoreType.DMA((2 * count,))],
        name="join_pages",
    )(targets, even, odd)


INTERPRET = False
LOG2E = 1.4426950408889634
ROWS = 512
BLOCKS = ROWS // SPAN
CONV_COLS = 512
CHUNK = 256
HALO = 16
TERMS = 3
SENT = STATE + 16
HEADS_STEP = 4
STEP_COLS = HEADS_STEP * HEAD_DIM
READ_COLS = 512
NORM_ROWS = 128
PER_GROUP = HEADS // GROUPS
GROUP_COLS = PER_GROUP * HEAD_DIM


def conv_kernel(halo_ref, tok_ref, weight_ref, taps_ref, bias_ref, mask_ref, out_ref, raw_ref):
    masks = [mask_ref[:, k : k + 1] for k in range(KCONV - 1)]
    for part in range(CONV_COLS // CHUNK):
        cols = slice(part * CHUNK, (part + 1) * CHUNK)
        weight = weight_ref[cols, :]
        dims = (((1,), (1,)), ((), ()))
        raw_ref[part, :HALO, :] = (
            lax.dot_general(halo_ref[...], weight, dims, preferred_element_type=jnp.float32)
            .astype(jnp.bfloat16)
            .astype(jnp.float32)
        )
        raw_ref[part, HALO:, :] = (
            lax.dot_general(tok_ref[...], weight, dims, preferred_element_type=jnp.float32)
            .astype(jnp.bfloat16)
            .astype(jnp.float32)
        )
    for part in range(CONV_COLS // CHUNK):
        cols = slice(part * CHUNK, (part + 1) * CHUNK)
        summed = bias_ref[:, cols] + taps_ref[KCONV - 1 : KCONV, cols] * raw_ref[part, HALO:, :]
        for k in range(KCONV - 1):
            start = HALO - (KCONV - 1) + k
            summed = (
                summed
                + (taps_ref[k : k + 1, cols] * raw_ref[part, start : start + ROWS, :]) * masks[k]
            )
        out_ref[:, cols] = (summed * (0.5 + 0.5 * jnp.tanh(0.5 * summed))).astype(jnp.bfloat16)


def project_conv(halo, tokens, weight, taps, bias, masks):
    width = weight.shape[0]
    return pl.pallas_call(
        conv_kernel,
        grid=(width // CONV_COLS,),
        out_shape=jax.ShapeDtypeStruct((ROWS, width), jnp.bfloat16),
        in_specs=[
            pl.BlockSpec((HALO, D), lambda n: (0, 0)),
            pl.BlockSpec((ROWS, D), lambda n: (0, 0)),
            pl.BlockSpec((CONV_COLS, D), lambda n: (n, 0)),
            pl.BlockSpec((KCONV, CONV_COLS), lambda n: (0, n)),
            pl.BlockSpec((1, CONV_COLS), lambda n: (0, n)),
            pl.BlockSpec((ROWS, KCONV - 1), lambda n: (0, 0)),
        ],
        out_specs=pl.BlockSpec((ROWS, CONV_COLS), lambda n: (0, n)),
        scratch_shapes=[pltpu.VMEM((CONV_COLS // CHUNK, HALO + ROWS, CHUNK), jnp.float32)],
        cost_estimate=pl.CostEstimate(
            flops=2 * (ROWS + HALO) * D * width,
            transcendentals=ROWS * width,
            bytes_accessed=2 * (ROWS * D + width * D + ROWS * width),
        ),
        name="project_conv",
        interpret=INTERPRET,
    )(halo, tokens, weight, taps, bias, masks)


def spread_heads(values, first_head, columns):
    upper = values.astype(jnp.bfloat16)
    lower = (values - upper.astype(jnp.float32)).astype(jnp.bfloat16)
    head = lax.broadcasted_iota(jnp.int32, (HEADS, columns), 0)
    column = lax.broadcasted_iota(jnp.int32, (HEADS, columns), 1)
    chosen = (head == first_head + column // HEAD_DIM).astype(jnp.bfloat16)
    return jnp.dot(upper, chosen, preferred_element_type=jnp.float32) + jnp.dot(
        lower, chosen, preferred_element_type=jnp.float32
    )


def state_kernel(first_ref, second_ref, b_ref, tail_ref, row_ref, gained_ref, local_ref):
    for group, x_ref in enumerate((first_ref, second_ref)):
        cols = slice(group * GROUP_COLS, (group + 1) * GROUP_COLS)
        tail = spread_heads(tail_ref[...], group * PER_GROUP, GROUP_COLS)
        weighted = (x_ref[...].astype(jnp.float32) * tail).astype(jnp.bfloat16)
        gained = [
            lax.dot_general(
                b_ref[b * SPAN : (b + 1) * SPAN, group * STATE : (group + 1) * STATE],
                weighted[b * SPAN : (b + 1) * SPAN],
                (((0,), (0,)), ((), ())),
                preferred_element_type=jnp.float32,
            )
            for b in range(BLOCKS)
        ]
        gained_ref[:, cols] = gained[0]
        local_ref[:STATE, cols] = (row_ref[1:2, cols] * gained[0] + gained[1]).astype(jnp.bfloat16)
        left = row_ref[0:1, cols] * row_ref[1:2, cols]
        row = lax.broadcasted_iota(jnp.int32, (SENT - STATE, GROUP_COLS), 0)
        terms = jnp.zeros((SENT - STATE, GROUP_COLS), jnp.float32)
        for at in range(TERMS):
            term = left.astype(jnp.bfloat16).astype(jnp.float32)
            terms = jnp.where(row == at, term, terms)
            left = left - term
        local_ref[STATE:, cols] = terms.astype(jnp.bfloat16)


def block_states(first, second, tail, rows):
    return pl.pallas_call(
        state_kernel,
        grid=(1,),
        out_shape=[
            jax.ShapeDtypeStruct((STATE, HALF), jnp.float32),
            jax.ShapeDtypeStruct((SENT, HALF), jnp.bfloat16),
        ],
        in_specs=[
            pl.BlockSpec((ROWS, GROUP_COLS), lambda i: (0, 0)),
            pl.BlockSpec((ROWS, GROUP_COLS), lambda i: (0, 0)),
            pl.BlockSpec((ROWS, BC), lambda i: (0, GROUP_COLS // BC)),
            pl.BlockSpec((ROWS, HEADS), lambda i: (0, 0)),
            pl.BlockSpec((8, HALF), lambda i: (0, 0)),
        ],
        out_specs=[
            pl.BlockSpec((STATE, HALF), lambda i: (0, 0)),
            pl.BlockSpec((SENT, HALF), lambda i: (0, 0)),
        ],
        cost_estimate=pl.CostEstimate(
            flops=2 * ROWS * HALF * STATE, transcendentals=0, bytes_accessed=4 << 20
        ),
        name="block_states",
        interpret=INTERPRET,
    )(first, second, first, tail, rows)


def mixing_kernel(x_ref, b_ref, c_ref, decay_ref, seg_ref, out_ref, scores_ref, bias_ref):
    @pl.when(pl.program_id(0) == 0)
    def _():
        at = lax.broadcasted_iota(jnp.int32, (SPAN, SPAN), 0)
        source = lax.broadcasted_iota(jnp.int32, (SPAN, SPAN), 1)
        for b in range(BLOCKS):
            rows = slice(b * SPAN, (b + 1) * SPAN)
            scores_ref[b] = lax.dot_general(
                c_ref[rows, :],
                b_ref[rows, :],
                (((1,), (1,)), ((), ())),
                preferred_element_type=jnp.float32,
            )
            across = seg_ref[:, rows]
            down = across.T[:, 0:1]
            allowed = (down == across[0:1, :]) & (at >= source)
            bias_ref[b] = jnp.where(allowed, 0.0, -1e30)

    half = SPAN // 2
    lane = lax.broadcasted_iota(jnp.int32, (half, 2 * HEAD_DIM), 1)
    for b in range(BLOCKS):
        decay = decay_ref[0, :, b * SPAN : (b + 1) * SPAN]
        down = decay.T
        for pair in range(HEADS_STEP // 2):
            cols = slice(pair * 2 * HEAD_DIM, (pair + 1) * 2 * HEAD_DIM)
            for part in range(2):
                reach = (part + 1) * half
                rows = slice(part * half, reach)
                found = []
                for head in (2 * pair, 2 * pair + 1):
                    spread = (
                        down[rows, head : head + 1]
                        - decay[HEADS_STEP + head : HEADS_STEP + head + 1, :reach]
                    )
                    mixing = (
                        jnp.exp2(spread + bias_ref[b, rows, :reach]) * scores_ref[b, rows, :reach]
                    ).astype(jnp.bfloat16)
                    found.append(
                        jnp.dot(
                            mixing,
                            x_ref[b * SPAN : b * SPAN + reach, cols],
                            preferred_element_type=jnp.float32,
                        )
                    )
                out_ref[b * SPAN + part * half : b * SPAN + reach, cols] = jnp.where(
                    lane < HEAD_DIM, found[0], found[1]
                )


def mix_blocks(x_out, bc_out, group, decay, seg):
    steps = PER_GROUP // HEADS_STEP
    at_b = GROUP_COLS // STATE + group
    return pl.pallas_call(
        mixing_kernel,
        grid=(steps,),
        out_shape=jax.ShapeDtypeStruct((ROWS, GROUP_COLS), jnp.float32),
        in_specs=[
            pl.BlockSpec((ROWS, STEP_COLS), lambda p: (0, p)),
            pl.BlockSpec((ROWS, STATE), lambda p: (0, at_b)),
            pl.BlockSpec((ROWS, STATE), lambda p: (0, at_b + GROUPS)),
            pl.BlockSpec((1, 8, ROWS), lambda p: (group * steps + p, 0, 0)),
            pl.BlockSpec((8, ROWS), lambda p: (0, 0)),
        ],
        out_specs=pl.BlockSpec((ROWS, STEP_COLS), lambda p: (0, p)),
        scratch_shapes=[pltpu.VMEM((BLOCKS, SPAN, SPAN), jnp.float32)] * 2,
        cost_estimate=pl.CostEstimate(
            flops=2 * ROWS * SPAN * GROUP_COLS,
            transcendentals=ROWS * SPAN * PER_GROUP,
            bytes_accessed=4 << 20,
        ),
        name="mix_blocks",
        interpret=INTERPRET,
    )(x_out, bc_out, bc_out, decay, seg)


def readout_kernel(
    y_ref, x_ref, c_ref, gained_ref, states_ref, factor_ref, row_ref, out_ref, power_ref, part_ref, *, group
):
    at = pl.program_id(0)
    incoming = jnp.zeros((STATE, READ_COLS), jnp.float32)
    for peer in range(states_ref.shape[0] - 1):
        terms = states_ref[peer, STATE:, :].astype(jnp.float32)
        through = (terms[0:1] + terms[1:2]) + terms[2:3]
        after = through * incoming + states_ref[peer, :STATE, :].astype(jnp.float32)
        incoming = jnp.where(row_ref[4 + peer : 5 + peer, :] > 0.5, after, incoming)
    second = row_ref[0:1, :] * incoming + gained_ref[...]
    first_head = group * PER_GROUP + at * (READ_COLS // HEAD_DIM)
    factor = spread_heads(factor_ref[...], first_head, READ_COLS)

    @pl.when(at == 0)
    def _():
        part_ref[...] = jnp.zeros_like(part_ref)

    for b, state in enumerate((incoming, second)):
        rows = slice(b * SPAN, (b + 1) * SPAN)
        readout = jnp.dot(
            c_ref[rows, :], state.astype(jnp.bfloat16), preferred_element_type=jnp.float32
        )
        combined = (
            y_ref[rows, :]
            + readout * factor[rows]
            + row_ref[2:3, :] * x_ref[rows, :].astype(jnp.float32)
        )
        out_ref[rows, :] = combined
        squared = combined * combined
        total = squared[:, :128]
        for tile in range(1, READ_COLS // 128):
            total = total + squared[:, tile * 128 : (tile + 1) * 128]
        part_ref[rows, :] += total

    @pl.when(at == GROUP_COLS // READ_COLS - 1)
    def _():
        power_ref[...] = jnp.sum(part_ref[...].T, axis=0, keepdims=True)


def read_states(mixed, x_out, bc_out, group, gained, states, factor, rows):
    steps = GROUP_COLS // READ_COLS
    peers = states.shape[0]
    return pl.pallas_call(
        partial(readout_kernel, group=group),
        grid=(steps,),
        out_shape=[
            jax.ShapeDtypeStruct((ROWS, GROUP_COLS), jnp.float32),
            jax.ShapeDtypeStruct((1, ROWS), jnp.float32),
        ],
        in_specs=[
            pl.BlockSpec((ROWS, READ_COLS), lambda p: (0, p)),
            pl.BlockSpec((ROWS, READ_COLS), lambda p: (0, p)),
            pl.BlockSpec((ROWS, STATE), lambda p: (0, GROUP_COLS // STATE + GROUPS + group)),
            pl.BlockSpec((STATE, READ_COLS), lambda p: (0, group * steps + p)),
            pl.BlockSpec((peers, SENT, READ_COLS), lambda p: (0, 0, group * steps + p)),
            pl.BlockSpec((ROWS, HEADS), lambda p: (0, 0)),
            pl.BlockSpec((8, READ_COLS), lambda p: (0, group * steps + p)),
        ],
        out_specs=[
            pl.BlockSpec((ROWS, READ_COLS), lambda p: (0, p)),
            pl.BlockSpec((1, ROWS), lambda p: (0, 0)),
        ],
        scratch_shapes=[pltpu.VMEM((ROWS, 128), jnp.float32)],
        cost_estimate=pl.CostEstimate(
            flops=2 * ROWS * STATE * GROUP_COLS, transcendentals=0, bytes_accessed=7 << 20
        ),
        name="read_states",
        interpret=INTERPRET,
    )(mixed, x_out, bc_out, gained, states, factor, rows)


def norm_kernel(first_ref, second_ref, power_ref, gain_ref, out_ref):
    mean = jnp.broadcast_to(power_ref[...], (8, NORM_ROWS)) / INNER
    scale = lax.rsqrt(mean + 1e-05).T[:, 0:1]
    for group, rows_ref in enumerate((first_ref, second_ref)):
        cols = slice(group * GROUP_COLS, (group + 1) * GROUP_COLS)
        out_ref[:, cols] = (rows_ref[...] * scale * gain_ref[:, cols]).astype(jnp.bfloat16)


def normalize(first, second, power, gain):
    return pl.pallas_call(
        norm_kernel,
        grid=(ROWS // NORM_ROWS,),
        out_shape=jax.ShapeDtypeStruct((ROWS, HALF), jnp.bfloat16),
        in_specs=[
            pl.BlockSpec((NORM_ROWS, GROUP_COLS), lambda i: (i, 0)),
            pl.BlockSpec((NORM_ROWS, GROUP_COLS), lambda i: (i, 0)),
            pl.BlockSpec((1, NORM_ROWS), lambda i: (0, i)),
            pl.BlockSpec((1, HALF), lambda i: (0, 0)),
        ],
        out_specs=pl.BlockSpec((NORM_ROWS, HALF), lambda i: (i, 0)),
        cost_estimate=pl.CostEstimate(
            flops=2 * ROWS * HALF, transcendentals=ROWS, bytes_accessed=6 << 20
        ),
        name="normalize",
        interpret=INTERPRET,
    )(first, second, power, gain)


def prepare(tokens, labels, step_weight, step_bias, decay_rate):
    step_raw = jnp.dot(tokens, step_weight, preferred_element_type=jnp.float32).astype(jnp.bfloat16)
    step_size = jax.nn.softplus(step_raw.astype(jnp.float32) + step_bias[None, :])
    seg = labels[KCONV - 1 :]
    change = (-step_size * decay_rate[None, :]).reshape(BLOCKS, SPAN, HEADS)
    log_decay = jnp.cumsum(change, axis=1)
    last = log_decay[:, SPAN - 1]
    seg_blocks = seg.reshape(BLOCKS, SPAN)
    final = seg_blocks[:, SPAN - 1]
    before = jnp.concatenate([labels[KCONV - 2][None], final[:-1]])
    tail = jnp.where(
        (seg_blocks == final[:, None])[:, :, None], jnp.exp(last[:, None] - log_decay), 0.0
    ) * step_size.reshape(BLOCKS, SPAN, HEADS)
    factor = jnp.where((seg_blocks == before[:, None])[:, :, None], jnp.exp(log_decay), 0.0)
    passing = jnp.where((final == before)[:, None], jnp.exp(last), 0.0)
    masks = jnp.stack(
        [(labels[k : k + ROWS] == seg).astype(jnp.float32) for k in range(KCONV - 1)], axis=1
    )
    scaled = (log_decay * LOG2E).reshape(ROWS, HEADS).T
    sized = scaled - jnp.log2(step_size).T
    decay = jnp.concatenate(
        [
            scaled.reshape(HEADS // HEADS_STEP, HEADS_STEP, ROWS),
            sized.reshape(HEADS // HEADS_STEP, HEADS_STEP, ROWS),
        ],
        axis=1,
    )
    seg_rows = jnp.broadcast_to(seg.astype(jnp.float32)[None, :], (8, ROWS))
    return dict(
        tail=tail.reshape(ROWS, HEADS),
        factor=factor.reshape(ROWS, HEADS),
        passing=passing,
        masks=masks,
        decay=decay,
        seg=seg_rows,
    )


def over_columns(values):
    return jnp.repeat(values, HEAD_DIM, axis=-1)


def per_device(
    stream_tokens,
    xbc_weight,
    step_weight,
    conv_weight,
    conv_bias,
    step_bias,
    decay_rate,
    skip_gain,
    norm_gain,
    segment_ids,
    page_target,
):
    request_groups = lax.axis_size("chip") * CORES
    tok_rows = stream_tokens.shape[0]
    page_rows = tok_rows // request_groups
    seq_at, core = lax.axis_index("seq"), lax.axis_index("core")
    flat = (seq_at * lax.axis_size("chip") + lax.axis_index("chip")) * CORES + core
    swap = [(0, 1), (1, 0)]
    peers = lax.axis_size("seq")
    onward = [(i, i + 1) for i in range(peers - 1)]

    targets = page_target[0]
    pages = scatter_pages(stream_tokens.reshape(request_groups, page_rows, D), targets)
    own = lax.all_to_all(pages, REQ, split_axis=0, concat_axis=0, tiled=True)
    own, own_ids = lax.optimization_barrier((own, segment_ids))
    other = lax.ppermute(own, "core", swap)
    other_ids = lax.ppermute(own_ids, "core", swap)

    def in_order(first, second):
        return [jnp.where(core == 0, first, second), jnp.where(core == 0, second, first)]

    tokens = [blocks.reshape(tok_rows, D) for blocks in in_order(own, other)]
    ids = in_order(own_ids, other_ids)
    halos = lax.ppermute(jnp.stack([rows[tok_rows - HALO :] for rows in tokens]), "seq", onward)

    pairs, picks = weight_moves()
    piece = xbc_weight.T.reshape(PIECE, UNIT, D)
    arrived = jnp.concatenate([lax.ppermute(piece, ALL, moves) for moves in pairs], axis=0)
    mine = jnp.asarray(picks)[flat]
    early = PARTS[0] // UNIT // RANKS
    first_units = pick_units(arrived, mine[:early])
    first_units, rest = lax.optimization_barrier((first_units, mine[early:]))
    weights = [
        lax.all_gather(units.reshape(-1, D), ("seq", "chip"), axis=0, tiled=True)
        for units in (first_units, pick_units(arrived, rest))
    ]

    def columns(values):
        x_cols = lax.dynamic_slice_in_dim(values, core * HALF, HALF, axis=-1)
        early = jnp.concatenate(
            [
                x_cols[:, : HALF // GROUPS],
                lax.dynamic_slice_in_dim(values, INNER + core * BC, BC, axis=-1),
                lax.dynamic_slice_in_dim(values, INNER + CORES * BC + core * BC, BC, axis=-1),
            ],
            axis=-1,
        )
        return early, x_cols[:, HALF // GROUPS :]

    def heads(values):
        return lax.dynamic_slice_in_dim(values, core * HEADS, HEADS, axis=-1)

    def labels(ids):
        padded = jnp.concatenate([jnp.full((KCONV - 1,), -1, jnp.int32), ids[0]])
        return lax.dynamic_slice_in_dim(padded, seq_at * tok_rows, tok_rows + KCONV - 1)

    taps, bias = columns(conv_weight), columns(conv_bias[None, :])
    step_half, step_shift, rate = heads(step_weight), heads(step_bias), heads(decay_rate)
    gain = lax.dynamic_slice_in_dim(norm_gain[None, :], core * HALF, HALF, axis=-1)
    ahead = (jnp.arange(peers) < seq_at).astype(jnp.float32)
    fixed_rows = jnp.concatenate(
        [
            over_columns(heads(skip_gain)[None, :]),
            jnp.zeros((1, HALF), jnp.float32),
            jnp.broadcast_to(ahead[:, None], (peers, HALF)),
        ],
        axis=0,
    )

    ready = [prepare(tokens[q], labels(ids[q]), step_half, step_shift, rate) for q in range(CORES)]

    def convolve(q, part):
        return project_conv(
            halos[q], tokens[q], weights[part], taps[part], bias[part], ready[q]["masks"]
        )

    early = [convolve(q, 0) for q in range(CORES)]
    mixed = [[mix_blocks(early[q], early[q], 0, ready[q]["decay"], ready[q]["seg"])] for q in range(CORES)]
    weights[1], early, mixed = lax.optimization_barrier((weights[1], early, mixed))
    late, rows, gained, every = [], [], [], []
    for q in range(CORES):
        late.append(convolve(q, 1))
        rows.append(jnp.concatenate([over_columns(ready[q]["passing"]), fixed_rows], axis=0))
        one, local = block_states(early[q], late[q], ready[q]["tail"], rows[q])
        gained.append(one)
        every.append(lax.all_gather(local, "seq"))
    for q in range(CORES):
        mixed[q].append(mix_blocks(late[q], early[q], 1, ready[q]["decay"], ready[q]["seg"]))

    returned = []
    normed = None
    for q in range(CORES):
        if q > 0:
            normed, mixed[q] = lax.optimization_barrier((normed, mixed[q]))
            returned.append(normed)
        parts = [
            read_states(
                mixed[q][group],
                (early, late)[group][q],
                early[q],
                group,
                gained[q],
                every[q],
                ready[q]["factor"],
                rows[q],
            )
            for group in range(GROUPS)
        ]
        power = parts[0][1] + parts[1][1]
        power = power + lax.ppermute(power, "core", swap)
        normed = normalize(parts[0][0], parts[1][0], power, gain)
    returned.append(normed)
    even, odd = [
        lax.all_to_all(
            rows_out.reshape(request_groups, page_rows, HALF),
            REQ,
            split_axis=0,
            concat_axis=0,
            tiled=True,
        )
        for rows_out in returned
    ]
    return join_pages(even, odd, targets).reshape(tok_rows, INNER)


def solution(mesh):
    chips = mesh.shape["req"] // CORES
    by_core = Mesh(
        mesh.devices.reshape(mesh.shape["seq"], chips, CORES), ("seq", "chip", "core")
    )
    in_specs = (
        P(ALL, None),
        P(None, ALL),
        P(),
        P(),
        P(),
        P(),
        P(),
        P(),
        P(),
        P(REQ, None),
        P(ALL, None),
    )
    return jax.shard_map(
        per_device, mesh=by_core, in_specs=in_specs, out_specs=P(ALL, None), check_vma=False
    )
```

```python
from functools import partial

import jax
import jax.numpy as jnp
from jax import lax
from jax.experimental import pallas as pl
from jax.experimental.pallas import tpu as pltpu
from jax.sharding import Mesh, PartitionSpec as P

HEAD_DIM = 64
STATE = 128
KCONV = 4
SPAN = 256
INNER = 4096
D = 2048
CORES = 2
HEADS = 32
GROUPS = 2
HALF = 2048
BC = GROUPS * STATE
OWN = HALF + 2 * BC

ALL = ("seq", "chip", "core")
REQ = ("chip", "core")


def move(index_ref, source_ref, out_ref, sems, *, places):
    copies = []
    for k, (source, target) in enumerate(places(index_ref)):
        copies.append(
            pltpu.make_async_copy(source_ref.at[source], out_ref.at[target], sems.at[k])
        )
    for copy in copies:
        copy.start()
    for copy in copies:
        copy.wait()


def scatter_pages(pages, targets):
    count = pages.shape[0]
    return pl.pallas_call(
        partial(move, places=lambda index: [(k, index[k]) for k in range(count)]),
        out_shape=jax.ShapeDtypeStruct(pages.shape, pages.dtype),
        in_specs=[pl.BlockSpec(memory_space=pltpu.SMEM), pl.BlockSpec(memory_space=pl.ANY)],
        out_specs=pl.BlockSpec(memory_space=pltpu.VMEM),
        scratch_shapes=[pltpu.SemaphoreType.DMA((count,))],
        name="scatter_pages",
    )(targets, pages)


def join_kernel(target_ref, even_ref, odd_ref, out_ref, sems):
    count = even_ref.shape[0]

    def copy(pages, page, k, half):
        return pltpu.make_async_copy(
            pages.at[page], out_ref.at[k, :, pl.ds(half * HALF, HALF)], sems.at[CORES * k + half]
        )

    for k in range(count):
        group = target_ref[k]
        odd = group % CORES
        for which, pages in enumerate((even_ref, odd_ref)):

            @pl.when(odd == which)
            def _():
                for half in range(CORES):
                    copy(pages, group - odd + half, k, half).start()

    for k in range(count):
        for half in range(CORES):
            copy(even_ref, 0, k, half).wait()


def join_pages(even, odd, targets):
    count, rows, width = even.shape
    return pl.pallas_call(
        join_kernel,
        out_shape=jax.ShapeDtypeStruct((count, rows, 2 * width), even.dtype),
        in_specs=[pl.BlockSpec(memory_space=pltpu.SMEM)] + [pl.BlockSpec(memory_space=pl.ANY)] * 2,
        out_specs=pl.BlockSpec(memory_space=pltpu.VMEM),
        scratch_shapes=[pltpu.SemaphoreType.DMA((2 * count,))],
        name="join_pages",
    )(targets, even, odd)


INTERPRET = False
LOG2E = 1.4426950408889634
ROWS = 512
BLOCKS = ROWS // SPAN
CONV_COLS = 512
CHUNK = 256
HALO = 16
TERMS = 3
SENT = STATE + 16
HEADS_STEP = 4
STEP_COLS = HEADS_STEP * HEAD_DIM
PER_GROUP = HEADS // GROUPS
GROUP_COLS = PER_GROUP * HEAD_DIM


def conv_kernel(
    core_ref, halo_ref, tok_ref, left_ref, right_ref, taps_ref, bias_ref, mask_ref, out_ref, raw_ref
):
    del core_ref
    masks = [mask_ref[:, k : k + 1] for k in range(KCONV - 1)]
    for part, weight_ref in enumerate((left_ref, right_ref)):
        dims = (((1,), (1,)), ((), ()))
        raw_ref[part, :HALO, :] = (
            lax.dot_general(
                halo_ref[...], weight_ref[...], dims, preferred_element_type=jnp.float32
            )
            .astype(jnp.bfloat16)
            .astype(jnp.float32)
        )
        raw_ref[part, HALO:, :] = (
            lax.dot_general(tok_ref[...], weight_ref[...], dims, preferred_element_type=jnp.float32)
            .astype(jnp.bfloat16)
            .astype(jnp.float32)
        )
    for part in range(CONV_COLS // CHUNK):
        cols = slice(part * CHUNK, (part + 1) * CHUNK)
        summed = bias_ref[:, cols] + taps_ref[KCONV - 1 : KCONV, cols] * raw_ref[part, HALO:, :]
        for k in range(KCONV - 1):
            start = HALO - (KCONV - 1) + k
            summed = (
                summed
                + (taps_ref[k : k + 1, cols] * raw_ref[part, start : start + ROWS, :]) * masks[k]
            )
        out_ref[:, cols] = (summed * (0.5 + 0.5 * jnp.tanh(0.5 * summed))).astype(jnp.bfloat16)


def project_conv(core, halo, tokens, weight, taps, bias, masks):
    x_steps = HALF // CONV_COLS

    def chunk(right):
        def at(n, core_ref):
            x_chunk = core_ref[0] * (HALF // CHUNK) + 2 * n + right
            bc_chunk = INNER // CHUNK + right * CORES * BC // CHUNK + core_ref[0]
            return jnp.where(n < x_steps, x_chunk, bc_chunk), 0

        return pl.BlockSpec((CHUNK, D), at)

    return pl.pallas_call(
        conv_kernel,
        grid_spec=pltpu.PrefetchScalarGridSpec(
            num_scalar_prefetch=1,
            grid=(OWN // CONV_COLS,),
            in_specs=[
                pl.BlockSpec((HALO, D), lambda n, core_ref: (0, 0)),
                pl.BlockSpec((ROWS, D), lambda n, core_ref: (0, 0)),
                chunk(0),
                chunk(1),
                pl.BlockSpec((KCONV, CONV_COLS), lambda n, core_ref: (0, n)),
                pl.BlockSpec((1, CONV_COLS), lambda n, core_ref: (0, n)),
                pl.BlockSpec((ROWS, KCONV - 1), lambda n, core_ref: (0, 0)),
            ],
            out_specs=pl.BlockSpec((ROWS, CONV_COLS), lambda n, core_ref: (0, n)),
            scratch_shapes=[pltpu.VMEM((CONV_COLS // CHUNK, HALO + ROWS, CHUNK), jnp.float32)],
        ),
        out_shape=jax.ShapeDtypeStruct((ROWS, OWN), jnp.bfloat16),
        cost_estimate=pl.CostEstimate(
            flops=2 * (ROWS + HALO) * D * OWN, transcendentals=ROWS * OWN, bytes_accessed=15 << 20
        ),
        name="project_conv",
        interpret=INTERPRET,
    )(core, halo, tokens, weight, weight, taps, bias, masks)


def spread_heads(values, first_head, columns):
    upper = values.astype(jnp.bfloat16)
    lower = (values - upper.astype(jnp.float32)).astype(jnp.bfloat16)
    head = lax.broadcasted_iota(jnp.int32, (HEADS, columns), 0)
    column = lax.broadcasted_iota(jnp.int32, (HEADS, columns), 1)
    chosen = (head == first_head + column // HEAD_DIM).astype(jnp.bfloat16)
    return jnp.dot(upper, chosen, preferred_element_type=jnp.float32) + jnp.dot(
        lower, chosen, preferred_element_type=jnp.float32
    )


def state_kernel(x_ref, b_ref, tail_ref, row_ref, gained_ref, local_ref):
    tail = spread_heads(tail_ref[...], pl.program_id(0) * PER_GROUP, GROUP_COLS)
    weighted = (x_ref[...].astype(jnp.float32) * tail).astype(jnp.bfloat16)
    gained = [
        lax.dot_general(
            b_ref[b * SPAN : (b + 1) * SPAN, :],
            weighted[b * SPAN : (b + 1) * SPAN],
            (((0,), (0,)), ((), ())),
            preferred_element_type=jnp.float32,
        )
        for b in range(BLOCKS)
    ]
    gained_ref[...] = gained[0]
    local_ref[:STATE, :] = (row_ref[1:2, :] * gained[0] + gained[1]).astype(jnp.bfloat16)
    left = row_ref[0:1, :] * row_ref[1:2, :]
    row = lax.broadcasted_iota(jnp.int32, (SENT - STATE, GROUP_COLS), 0)
    terms = jnp.zeros((SENT - STATE, GROUP_COLS), jnp.float32)
    for at in range(TERMS):
        term = left.astype(jnp.bfloat16).astype(jnp.float32)
        terms = jnp.where(row == at, term, terms)
        left = left - term
    local_ref[STATE:, :] = terms.astype(jnp.bfloat16)


def block_states(conv_out, tail, rows):
    return pl.pallas_call(
        state_kernel,
        grid=(GROUPS,),
        out_shape=[
            jax.ShapeDtypeStruct((STATE, HALF), jnp.float32),
            jax.ShapeDtypeStruct((SENT, HALF), jnp.bfloat16),
        ],
        in_specs=[
            pl.BlockSpec((ROWS, GROUP_COLS), lambda g: (0, g)),
            pl.BlockSpec((ROWS, STATE), lambda g: (0, HALF // STATE + g)),
            pl.BlockSpec((ROWS, HEADS), lambda g: (0, 0)),
            pl.BlockSpec((8, GROUP_COLS), lambda g: (0, g)),
        ],
        out_specs=[
            pl.BlockSpec((STATE, GROUP_COLS), lambda g: (0, g)),
            pl.BlockSpec((SENT, GROUP_COLS), lambda g: (0, g)),
        ],
        cost_estimate=pl.CostEstimate(
            flops=2 * ROWS * HALF * STATE, transcendentals=0, bytes_accessed=4 << 20
        ),
        name="block_states",
        interpret=INTERPRET,
    )(conv_out, conv_out, tail, rows)


def mixing_kernel(x_ref, b_ref, c_ref, decay_ref, seg_ref, out_ref, scores_ref, bias_ref):
    @pl.when(pl.program_id(1) == 0)
    def _():
        at = lax.broadcasted_iota(jnp.int32, (SPAN, SPAN), 0)
        source = lax.broadcasted_iota(jnp.int32, (SPAN, SPAN), 1)
        for b in range(BLOCKS):
            rows = slice(b * SPAN, (b + 1) * SPAN)
            scores_ref[b] = lax.dot_general(
                c_ref[rows, :],
                b_ref[rows, :],
                (((1,), (1,)), ((), ())),
                preferred_element_type=jnp.float32,
            )
            across = seg_ref[:, rows]
            down = across.T[:, 0:1]
            allowed = (down == across[0:1, :]) & (at >= source)
            bias_ref[b] = jnp.where(allowed, 0.0, -1e30)

    half = SPAN // 2
    lane = lax.broadcasted_iota(jnp.int32, (half, 2 * HEAD_DIM), 1)
    for b in range(BLOCKS):
        decay = decay_ref[0, :, b * SPAN : (b + 1) * SPAN]
        down = decay.T
        for pair in range(HEADS_STEP // 2):
            cols = slice(pair * 2 * HEAD_DIM, (pair + 1) * 2 * HEAD_DIM)
            for part in range(2):
                reach = (part + 1) * half
                rows = slice(part * half, reach)
                found = []
                for head in (2 * pair, 2 * pair + 1):
                    spread = (
                        down[rows, head : head + 1]
                        - decay[HEADS_STEP + head : HEADS_STEP + head + 1, :reach]
                    )
                    mixing = (
                        jnp.exp2(spread + bias_ref[b, rows, :reach]) * scores_ref[b, rows, :reach]
                    ).astype(jnp.bfloat16)
                    found.append(
                        jnp.dot(
                            mixing,
                            x_ref[b * SPAN : b * SPAN + reach, cols],
                            preferred_element_type=jnp.float32,
                        )
                    )
                out_ref[b * SPAN + part * half : b * SPAN + reach, cols] = jnp.where(
                    lane < HEAD_DIM, found[0], found[1]
                ).astype(jnp.bfloat16)


def mix_blocks(conv_out, decay, seg):
    steps = PER_GROUP // HEADS_STEP
    return pl.pallas_call(
        mixing_kernel,
        grid=(GROUPS, steps),
        out_shape=jax.ShapeDtypeStruct((ROWS, HALF), jnp.bfloat16),
        in_specs=[
            pl.BlockSpec((ROWS, STEP_COLS), lambda g, p: (0, g * steps + p)),
            pl.BlockSpec((ROWS, STATE), lambda g, p: (0, HALF // STATE + g)),
            pl.BlockSpec((ROWS, STATE), lambda g, p: (0, HALF // STATE + GROUPS + g)),
            pl.BlockSpec((1, 8, ROWS), lambda g, p: (g * steps + p, 0, 0)),
            pl.BlockSpec((8, ROWS), lambda g, p: (0, 0)),
        ],
        out_specs=pl.BlockSpec((ROWS, STEP_COLS), lambda g, p: (0, g * steps + p)),
        scratch_shapes=[pltpu.VMEM((BLOCKS, SPAN, SPAN), jnp.float32)] * 2,
        cost_estimate=pl.CostEstimate(
            flops=2 * ROWS * SPAN * HALF,
            transcendentals=ROWS * SPAN * HEADS,
            bytes_accessed=7 << 20,
        ),
        name="mix_blocks",
        interpret=INTERPRET,
    )(conv_out, conv_out, conv_out, decay, seg)


def readout_kernel(
    y_ref, x_ref, c_ref, gained_ref, states_ref, factor_ref, row_ref, out_ref, power_ref, part_ref
):
    steps = PER_GROUP // HEADS_STEP
    at = pl.program_id(0) * steps + pl.program_id(1)
    incoming = jnp.zeros((STATE, STEP_COLS), jnp.float32)
    for peer in range(states_ref.shape[0] - 1):
        terms = states_ref[peer, STATE:, :].astype(jnp.float32)
        through = (terms[0:1] + terms[1:2]) + terms[2:3]
        after = through * incoming + states_ref[peer, :STATE, :].astype(jnp.float32)
        incoming = jnp.where(row_ref[4 + peer : 5 + peer, :] > 0.5, after, incoming)
    second = row_ref[0:1, :] * incoming + gained_ref[...]
    factor = spread_heads(factor_ref[...], at * HEADS_STEP, STEP_COLS)

    @pl.when(at == 0)
    def _():
        part_ref[...] = jnp.zeros_like(part_ref)

    for b, state in enumerate((incoming, second)):
        rows = slice(b * SPAN, (b + 1) * SPAN)
        readout = jnp.dot(
            c_ref[rows, :], state.astype(jnp.bfloat16), preferred_element_type=jnp.float32
        )
        combined = (
            y_ref[rows, :].astype(jnp.float32)
            + readout * factor[rows]
            + row_ref[2:3, :] * x_ref[rows, :].astype(jnp.float32)
        )
        out_ref[rows, :] = combined.astype(jnp.bfloat16)
        squared = combined * combined
        part_ref[rows, :] += squared[:, :128] + squared[:, 128:]

    @pl.when(at == GROUPS * steps - 1)
    def _():
        power_ref[...] = jnp.sum(part_ref[...].T, axis=0, keepdims=True)


def read_states(mixed, conv_out, gained, states, factor, rows):
    steps = PER_GROUP // HEADS_STEP
    peers = states.shape[0]
    return pl.pallas_call(
        readout_kernel,
        grid=(GROUPS, steps),
        out_shape=[
            jax.ShapeDtypeStruct((ROWS, HALF), jnp.bfloat16),
            jax.ShapeDtypeStruct((1, ROWS), jnp.float32),
        ],
        in_specs=[
            pl.BlockSpec((ROWS, STEP_COLS), lambda g, p: (0, g * steps + p)),
            pl.BlockSpec((ROWS, STEP_COLS), lambda g, p: (0, g * steps + p)),
            pl.BlockSpec((ROWS, STATE), lambda g, p: (0, HALF // STATE + GROUPS + g)),
            pl.BlockSpec((STATE, STEP_COLS), lambda g, p: (0, g * steps + p)),
            pl.BlockSpec((peers, SENT, STEP_COLS), lambda g, p: (0, 0, g * steps + p)),
            pl.BlockSpec((ROWS, HEADS), lambda g, p: (0, 0)),
            pl.BlockSpec((8, STEP_COLS), lambda g, p: (0, g * steps + p)),
        ],
        out_specs=[
            pl.BlockSpec((ROWS, STEP_COLS), lambda g, p: (0, g * steps + p)),
            pl.BlockSpec((1, ROWS), lambda g, p: (0, 0)),
        ],
        scratch_shapes=[pltpu.VMEM((ROWS, 128), jnp.float32)],
        cost_estimate=pl.CostEstimate(
            flops=2 * ROWS * STATE * HALF, transcendentals=0, bytes_accessed=14 << 20
        ),
        name="read_states",
        interpret=INTERPRET,
    )(mixed, conv_out, conv_out, gained, states, factor, rows)


def prepare(tokens, labels, step_weight, step_bias, decay_rate):
    step_raw = jnp.dot(tokens, step_weight, preferred_element_type=jnp.float32).astype(jnp.bfloat16)
    step_size = jax.nn.softplus(step_raw.astype(jnp.float32) + step_bias[None, :])
    seg = labels[KCONV - 1 :]
    change = (-step_size * decay_rate[None, :]).reshape(BLOCKS, SPAN, HEADS)
    log_decay = jnp.cumsum(change, axis=1)
    last = log_decay[:, SPAN - 1]
    seg_blocks = seg.reshape(BLOCKS, SPAN)
    final = seg_blocks[:, SPAN - 1]
    before = jnp.concatenate([labels[KCONV - 2][None], final[:-1]])
    tail = jnp.where(
        (seg_blocks == final[:, None])[:, :, None], jnp.exp(last[:, None] - log_decay), 0.0
    ) * step_size.reshape(BLOCKS, SPAN, HEADS)
    factor = jnp.where((seg_blocks == before[:, None])[:, :, None], jnp.exp(log_decay), 0.0)
    passing = jnp.where((final == before)[:, None], jnp.exp(last), 0.0)
    masks = jnp.stack(
        [(labels[k : k + ROWS] == seg).astype(jnp.float32) for k in range(KCONV - 1)], axis=1
    )
    scaled = (log_decay * LOG2E).reshape(ROWS, HEADS).T
    sized = scaled - jnp.log2(step_size).T
    decay = jnp.concatenate(
        [
            scaled.reshape(HEADS // HEADS_STEP, HEADS_STEP, ROWS),
            sized.reshape(HEADS // HEADS_STEP, HEADS_STEP, ROWS),
        ],
        axis=1,
    )
    seg_rows = jnp.broadcast_to(seg.astype(jnp.float32)[None, :], (8, ROWS))
    return dict(
        tail=tail.reshape(ROWS, HEADS),
        factor=factor.reshape(ROWS, HEADS),
        passing=passing,
        masks=masks,
        decay=decay,
        seg=seg_rows,
    )


def over_columns(values):
    return jnp.repeat(values, HEAD_DIM, axis=-1)


def per_device(
    stream_tokens,
    xbc_weight,
    step_weight,
    conv_weight,
    conv_bias,
    step_bias,
    decay_rate,
    skip_gain,
    norm_gain,
    segment_ids,
    page_target,
):
    request_groups = lax.axis_size("chip") * CORES
    tok_rows = stream_tokens.shape[0]
    page_rows = tok_rows // request_groups
    seq_at, core = lax.axis_index("seq"), lax.axis_index("core")
    swap = [(0, 1), (1, 0)]
    peers = lax.axis_size("seq")
    onward = [(i, i + 1) for i in range(peers - 1)]

    targets = page_target[0]
    pages = scatter_pages(stream_tokens.reshape(request_groups, page_rows, D), targets)
    own = lax.all_to_all(pages, REQ, split_axis=0, concat_axis=0, tiled=True)
    own, own_ids = lax.optimization_barrier((own, segment_ids))
    other = lax.ppermute(own, "core", swap)
    other_ids = lax.ppermute(own_ids, "core", swap)

    def in_order(first, second):
        return [jnp.where(core == 0, first, second), jnp.where(core == 0, second, first)]

    tokens = [blocks.reshape(tok_rows, D) for blocks in in_order(own, other)]
    ids = in_order(own_ids, other_ids)
    halos = lax.ppermute(jnp.stack([rows[tok_rows - HALO :] for rows in tokens]), "seq", onward)

    weight = lax.all_gather(xbc_weight.T, ALL, axis=0, tiled=True)

    def columns(values):
        return jnp.concatenate(
            [
                lax.dynamic_slice_in_dim(values, core * HALF, HALF, axis=-1),
                lax.dynamic_slice_in_dim(values, INNER + core * BC, BC, axis=-1),
                lax.dynamic_slice_in_dim(values, INNER + CORES * BC + core * BC, BC, axis=-1),
            ],
            axis=-1,
        )

    def heads(values):
        return lax.dynamic_slice_in_dim(values, core * HEADS, HEADS, axis=-1)

    def labels(ids):
        padded = jnp.concatenate([jnp.full((KCONV - 1,), -1, jnp.int32), ids[0]])
        return lax.dynamic_slice_in_dim(padded, seq_at * tok_rows, tok_rows + KCONV - 1)

    taps, bias = columns(conv_weight), columns(conv_bias[None, :])
    step_half, step_shift, rate = heads(step_weight), heads(step_bias), heads(decay_rate)
    gain = lax.dynamic_slice_in_dim(norm_gain[None, :], core * HALF, HALF, axis=-1)
    ahead = (jnp.arange(peers) < seq_at).astype(jnp.float32)
    fixed_rows = jnp.concatenate(
        [
            over_columns(heads(skip_gain)[None, :]),
            jnp.zeros((1, HALF), jnp.float32),
            jnp.broadcast_to(ahead[:, None], (peers, HALF)),
        ],
        axis=0,
    )

    at_core = core.astype(jnp.int32)[None]
    ready, rows, conv_out, gained, every = [], [], [], [], []
    for q in range(CORES):
        one = prepare(tokens[q], labels(ids[q]), step_half, step_shift, rate)
        ready.append(one)
        rows.append(jnp.concatenate([over_columns(one["passing"]), fixed_rows], axis=0))
        conv_out.append(
            project_conv(at_core, halos[q], tokens[q], weight, taps, bias, one["masks"])
        )
        after_first, local = block_states(conv_out[q], one["tail"], rows[q])
        gained.append(after_first)
        every.append(lax.all_gather(local, "seq"))

    returned = []
    for q in range(CORES):
        decay = ready[q]["decay"]
        if q > 0:
            returned[0], decay = lax.optimization_barrier((returned[0], decay))
        mixed = mix_blocks(conv_out[q], decay, ready[q]["seg"])
        combined, power = read_states(
            mixed, conv_out[q], gained[q], every[q], ready[q]["factor"], rows[q]
        )
        power = power + lax.ppermute(power, "core", swap)
        scale = lax.rsqrt(power[0] / INNER + 1e-05)
        returned.append(
            (combined.astype(jnp.float32) * scale[:, None] * gain).astype(jnp.bfloat16)
        )
    even, odd = [
        lax.all_to_all(
            rows_out.reshape(request_groups, page_rows, HALF),
            REQ,
            split_axis=0,
            concat_axis=0,
            tiled=True,
        )
        for rows_out in returned
    ]
    return join_pages(even, odd, targets).reshape(tok_rows, INNER)


def solution(mesh):
    chips = mesh.shape["req"] // CORES
    by_core = Mesh(
        mesh.devices.reshape(mesh.shape["seq"], chips, CORES), ("seq", "chip", "core")
    )
    in_specs = (
        P(ALL, None),
        P(None, ALL),
        P(),
        P(),
        P(),
        P(),
        P(),
        P(),
        P(),
        P(REQ, None),
        P(ALL, None),
    )
    return jax.shard_map(
        per_device, mesh=by_core, in_specs=in_specs, out_specs=P(ALL, None), check_vma=False
    )
```

```python
from functools import partial

import jax
import jax.numpy as jnp
from jax import lax
from jax.experimental import pallas as pl
from jax.experimental.pallas import tpu as pltpu
from jax.sharding import Mesh, PartitionSpec as P

HEAD_DIM = 64
STATE = 128
KCONV = 4
SPAN = 256
INNER = 4096
D = 2048
CORES = 2
HEADS = 32
GROUPS = 2
HALF = 2048
BC = GROUPS * STATE
OWN = HALF + 2 * BC

ALL = ("seq", "chip", "core")
REQ = ("chip", "core")


def move(index_ref, source_ref, out_ref, sems, *, places):
    copies = []
    for k, (source, target) in enumerate(places(index_ref)):
        copies.append(
            pltpu.make_async_copy(source_ref.at[source], out_ref.at[target], sems.at[k])
        )
    for copy in copies:
        copy.start()
    for copy in copies:
        copy.wait()


def scatter_pages(pages, targets):
    count = pages.shape[0]
    return pl.pallas_call(
        partial(move, places=lambda index: [(k, index[k]) for k in range(count)]),
        out_shape=jax.ShapeDtypeStruct(pages.shape, pages.dtype),
        in_specs=[pl.BlockSpec(memory_space=pltpu.SMEM), pl.BlockSpec(memory_space=pl.ANY)],
        out_specs=pl.BlockSpec(memory_space=pltpu.VMEM),
        scratch_shapes=[pltpu.SemaphoreType.DMA((count,))],
        name="scatter_pages",
    )(targets, pages)


def join_kernel(target_ref, even_ref, odd_ref, out_ref, held_ref, read_sems, write_sems):
    count = even_ref.shape[0]

    def read(pages, page, k, half):
        return pltpu.make_async_copy(
            pages.at[page],
            held_ref.at[k, :, pl.ds(half * HALF, HALF)],
            read_sems.at[CORES * k + half],
        )

    def write(k):
        return pltpu.make_async_copy(held_ref.at[k], out_ref.at[k], write_sems.at[k])

    for k in range(count):
        group = target_ref[k]
        odd = group % CORES
        for which, pages in enumerate((even_ref, odd_ref)):

            @pl.when(odd == which)
            def _():
                for half in range(CORES):
                    read(pages, group - odd + half, k, half).start()

    for k in range(count):
        for half in range(CORES):
            read(even_ref, 0, k, half).wait()
        write(k).start()
    for k in range(count):
        write(k).wait()


def join_pages(even, odd, targets):
    count, rows, width = even.shape
    return pl.pallas_call(
        join_kernel,
        out_shape=jax.ShapeDtypeStruct((count, rows, 2 * width), even.dtype),
        in_specs=[pl.BlockSpec(memory_space=pltpu.SMEM)] + [pl.BlockSpec(memory_space=pl.ANY)] * 2,
        out_specs=pl.BlockSpec(memory_space=pl.ANY),
        scratch_shapes=[
            pltpu.VMEM((count, rows, 2 * width), even.dtype),
            pltpu.SemaphoreType.DMA((CORES * count,)),
            pltpu.SemaphoreType.DMA((count,)),
        ],
        name="join_pages",
    )(targets, even, odd)


INTERPRET = False
LOG2E = 1.4426950408889634
ROWS = 512
BLOCKS = ROWS // SPAN
CONV_COLS = 512
CHUNK = 256
HALO = 16
TERMS = 3
SENT = STATE + 16
HEADS_STEP = 4
STEP_COLS = HEADS_STEP * HEAD_DIM
READ_COLS = 512
PER_GROUP = HEADS // GROUPS
GROUP_COLS = PER_GROUP * HEAD_DIM


def conv_kernel(
    core_ref, halo_ref, tok_ref, left_ref, right_ref, taps_ref, bias_ref, mask_ref, out_ref, raw_ref
):
    del core_ref
    masks = [mask_ref[:, k : k + 1] for k in range(KCONV - 1)]
    for part, weight_ref in enumerate((left_ref, right_ref)):
        dims = (((1,), (1,)), ((), ()))
        raw_ref[part, :HALO, :] = (
            lax.dot_general(
                halo_ref[...], weight_ref[...], dims, preferred_element_type=jnp.float32
            )
            .astype(jnp.bfloat16)
            .astype(jnp.float32)
        )
        raw_ref[part, HALO:, :] = (
            lax.dot_general(tok_ref[...], weight_ref[...], dims, preferred_element_type=jnp.float32)
            .astype(jnp.bfloat16)
            .astype(jnp.float32)
        )
    for part in range(CONV_COLS // CHUNK):
        cols = slice(part * CHUNK, (part + 1) * CHUNK)
        summed = bias_ref[:, cols] + taps_ref[KCONV - 1 : KCONV, cols] * raw_ref[part, HALO:, :]
        for k in range(KCONV - 1):
            start = HALO - (KCONV - 1) + k
            summed = (
                summed
                + (taps_ref[k : k + 1, cols] * raw_ref[part, start : start + ROWS, :]) * masks[k]
            )
        out_ref[:, cols] = (summed * (0.5 + 0.5 * jnp.tanh(0.5 * summed))).astype(jnp.bfloat16)


def project_conv(core, halo, tokens, weight, taps, bias, masks):
    x_steps = HALF // CONV_COLS

    def chunk(right):
        def at(n, core_ref):
            x_chunk = core_ref[0] * (HALF // CHUNK) + 2 * n + right
            bc_chunk = INNER // CHUNK + right * CORES * BC // CHUNK + core_ref[0]
            return jnp.where(n < x_steps, x_chunk, bc_chunk), 0

        return pl.BlockSpec((CHUNK, D), at)

    return pl.pallas_call(
        conv_kernel,
        grid_spec=pltpu.PrefetchScalarGridSpec(
            num_scalar_prefetch=1,
            grid=(OWN // CONV_COLS,),
            in_specs=[
                pl.BlockSpec((HALO, D), lambda n, core_ref: (0, 0)),
                pl.BlockSpec((ROWS, D), lambda n, core_ref: (0, 0)),
                chunk(0),
                chunk(1),
                pl.BlockSpec((KCONV, CONV_COLS), lambda n, core_ref: (0, n)),
                pl.BlockSpec((1, CONV_COLS), lambda n, core_ref: (0, n)),
                pl.BlockSpec((ROWS, KCONV - 1), lambda n, core_ref: (0, 0)),
            ],
            out_specs=pl.BlockSpec((ROWS, CONV_COLS), lambda n, core_ref: (0, n)),
            scratch_shapes=[pltpu.VMEM((CONV_COLS // CHUNK, HALO + ROWS, CHUNK), jnp.float32)],
        ),
        out_shape=jax.ShapeDtypeStruct((ROWS, OWN), jnp.bfloat16),
        cost_estimate=pl.CostEstimate(
            flops=2 * (ROWS + HALO) * D * OWN, transcendentals=ROWS * OWN, bytes_accessed=15 << 20
        ),
        name="project_conv",
        interpret=INTERPRET,
    )(core, halo, tokens, weight, weight, taps, bias, masks)


def spread_heads(terms, first_head, columns):
    head = lax.broadcasted_iota(jnp.int32, (2 * HEADS, columns), 0) % HEADS
    column = lax.broadcasted_iota(jnp.int32, (2 * HEADS, columns), 1)
    chosen = (head == first_head + column // HEAD_DIM).astype(jnp.bfloat16)
    return jnp.dot(terms, chosen, preferred_element_type=jnp.float32)


def two_terms(values):
    upper = lax.reduce_precision(values, 8, 7)
    return jnp.concatenate([upper, values - upper], axis=-1).astype(jnp.bfloat16)


def state_kernel(x_ref, b_ref, tail_ref, row_ref, gained_ref, local_ref):
    tail = spread_heads(tail_ref[...], pl.program_id(0) * PER_GROUP, GROUP_COLS)
    weighted = (x_ref[...].astype(jnp.float32) * tail).astype(jnp.bfloat16)
    gained = [
        lax.dot_general(
            b_ref[b * SPAN : (b + 1) * SPAN, :],
            weighted[b * SPAN : (b + 1) * SPAN],
            (((0,), (0,)), ((), ())),
            preferred_element_type=jnp.float32,
        )
        for b in range(BLOCKS)
    ]
    gained_ref[...] = gained[0]
    local_ref[:STATE, :] = (row_ref[1:2, :] * gained[0] + gained[1]).astype(jnp.bfloat16)
    left = row_ref[0:1, :] * row_ref[1:2, :]
    row = lax.broadcasted_iota(jnp.int32, (SENT - STATE, GROUP_COLS), 0)
    terms = jnp.zeros((SENT - STATE, GROUP_COLS), jnp.float32)
    for at in range(TERMS):
        term = left.astype(jnp.bfloat16).astype(jnp.float32)
        terms = jnp.where(row == at, term, terms)
        left = left - term
    local_ref[STATE:, :] = terms.astype(jnp.bfloat16)


def block_states(conv_out, tail, rows):
    return pl.pallas_call(
        state_kernel,
        grid=(GROUPS,),
        out_shape=[
            jax.ShapeDtypeStruct((STATE, HALF), jnp.float32),
            jax.ShapeDtypeStruct((SENT, HALF), jnp.bfloat16),
        ],
        in_specs=[
            pl.BlockSpec((ROWS, GROUP_COLS), lambda g: (0, g)),
            pl.BlockSpec((ROWS, STATE), lambda g: (0, HALF // STATE + g)),
            pl.BlockSpec((ROWS, 2 * HEADS), lambda g: (0, 0)),
            pl.BlockSpec((8, GROUP_COLS), lambda g: (0, g)),
        ],
        out_specs=[
            pl.BlockSpec((STATE, GROUP_COLS), lambda g: (0, g)),
            pl.BlockSpec((SENT, GROUP_COLS), lambda g: (0, g)),
        ],
        cost_estimate=pl.CostEstimate(
            flops=2 * ROWS * HALF * STATE, transcendentals=0, bytes_accessed=4 << 20
        ),
        name="block_states",
        interpret=INTERPRET,
    )(conv_out, conv_out, tail, rows)


def mixing_kernel(x_ref, b_ref, c_ref, decay_ref, seg_ref, out_ref, scores_ref, bias_ref):
    @pl.when(pl.program_id(1) == 0)
    def _():
        at = lax.broadcasted_iota(jnp.int32, (SPAN, SPAN), 0)
        source = lax.broadcasted_iota(jnp.int32, (SPAN, SPAN), 1)
        for b in range(BLOCKS):
            rows = slice(b * SPAN, (b + 1) * SPAN)
            scores_ref[b] = lax.dot_general(
                c_ref[rows, :],
                b_ref[rows, :],
                (((1,), (1,)), ((), ())),
                preferred_element_type=jnp.float32,
            )
            across = seg_ref[:, rows]
            down = across.T[:, 0:1]
            allowed = (down == across[0:1, :]) & (at >= source)
            bias_ref[b] = jnp.where(allowed, 0.0, -1e30)

    half = SPAN // 2
    lane = lax.broadcasted_iota(jnp.int32, (half, 2 * HEAD_DIM), 1)
    for b in range(BLOCKS):
        decay = decay_ref[0, :, b * SPAN : (b + 1) * SPAN]
        down = decay.T
        for pair in range(HEADS_STEP // 2):
            cols = slice(pair * 2 * HEAD_DIM, (pair + 1) * 2 * HEAD_DIM)
            for part in range(2):
                reach = (part + 1) * half
                rows = slice(part * half, reach)
                mixing = []
                for head in (2 * pair, 2 * pair + 1):
                    spread = (
                        down[rows, head : head + 1]
                        - decay[HEADS_STEP + head : HEADS_STEP + head + 1, :reach]
                    )
                    mixing.append(
                        (
                            jnp.exp2(spread + bias_ref[b, rows, :reach])
                            * scores_ref[b, rows, :reach]
                        ).astype(jnp.bfloat16)
                    )
                found = jnp.dot(
                    jnp.concatenate(mixing, axis=0),
                    x_ref[b * SPAN : b * SPAN + reach, cols],
                    preferred_element_type=jnp.float32,
                )
                out_ref[b * SPAN + part * half : b * SPAN + reach, cols] = jnp.where(
                    lane < HEAD_DIM, found[:half], found[half:]
                ).astype(jnp.bfloat16)


def mix_blocks(conv_out, decay, seg):
    steps = PER_GROUP // HEADS_STEP
    return pl.pallas_call(
        mixing_kernel,
        grid=(GROUPS, steps),
        out_shape=jax.ShapeDtypeStruct((ROWS, HALF), jnp.bfloat16),
        in_specs=[
            pl.BlockSpec((ROWS, STEP_COLS), lambda g, p: (0, g * steps + p)),
            pl.BlockSpec((ROWS, STATE), lambda g, p: (0, HALF // STATE + g)),
            pl.BlockSpec((ROWS, STATE), lambda g, p: (0, HALF // STATE + GROUPS + g)),
            pl.BlockSpec((1, 8, ROWS), lambda g, p: (g * steps + p, 0, 0)),
            pl.BlockSpec((8, ROWS), lambda g, p: (0, 0)),
        ],
        out_specs=pl.BlockSpec((ROWS, STEP_COLS), lambda g, p: (0, g * steps + p)),
        scratch_shapes=[pltpu.VMEM((BLOCKS, SPAN, SPAN), jnp.float32)] * 2,
        cost_estimate=pl.CostEstimate(
            flops=2 * ROWS * SPAN * HALF,
            transcendentals=ROWS * SPAN * HEADS,
            bytes_accessed=7 << 20,
        ),
        name="mix_blocks",
        interpret=INTERPRET,
    )(conv_out, conv_out, conv_out, decay, seg)


def readout_kernel(
    y_ref, x_ref, c_ref, gained_ref, states_ref, factor_ref, row_ref, out_ref, power_ref, part_ref
):
    steps = GROUP_COLS // READ_COLS
    at = pl.program_id(0) * steps + pl.program_id(1)
    incoming = jnp.zeros((STATE, READ_COLS), jnp.float32)
    for peer in range(states_ref.shape[0] - 1):
        terms = states_ref[peer, STATE:, :].astype(jnp.float32)
        through = (terms[0:1] + terms[1:2]) + terms[2:3]
        after = through * incoming + states_ref[peer, :STATE, :].astype(jnp.float32)
        incoming = jnp.where(row_ref[4 + peer : 5 + peer, :] > 0.5, after, incoming)
    second = row_ref[0:1, :] * incoming + gained_ref[...]
    factor = spread_heads(factor_ref[...], at * (READ_COLS // HEAD_DIM), READ_COLS)

    @pl.when(at == 0)
    def _():
        part_ref[...] = jnp.zeros_like(part_ref)

    for b, state in enumerate((incoming, second)):
        rows = slice(b * SPAN, (b + 1) * SPAN)
        readout = jnp.dot(
            c_ref[rows, :], state.astype(jnp.bfloat16), preferred_element_type=jnp.float32
        )
        combined = (
            y_ref[rows, :].astype(jnp.float32)
            + readout * factor[rows]
            + row_ref[2:3, :] * x_ref[rows, :].astype(jnp.float32)
        )
        out_ref[rows, :] = combined.astype(jnp.bfloat16)
        squared = combined * combined
        total = squared[:, :128]
        for tile in range(1, READ_COLS // 128):
            total = total + squared[:, tile * 128 : (tile + 1) * 128]
        part_ref[rows, :] += total

    @pl.when(at == GROUPS * steps - 1)
    def _():
        power_ref[...] = jnp.sum(part_ref[...].T, axis=0, keepdims=True)


def read_states(mixed, conv_out, gained, states, factor, rows):
    steps = GROUP_COLS // READ_COLS
    peers = states.shape[0]
    return pl.pallas_call(
        readout_kernel,
        grid=(GROUPS, steps),
        out_shape=[
            jax.ShapeDtypeStruct((ROWS, HALF), jnp.bfloat16),
            jax.ShapeDtypeStruct((1, ROWS), jnp.float32),
        ],
        in_specs=[
            pl.BlockSpec((ROWS, READ_COLS), lambda g, p: (0, g * steps + p)),
            pl.BlockSpec((ROWS, READ_COLS), lambda g, p: (0, g * steps + p)),
            pl.BlockSpec((ROWS, STATE), lambda g, p: (0, HALF // STATE + GROUPS + g)),
            pl.BlockSpec((STATE, READ_COLS), lambda g, p: (0, g * steps + p)),
            pl.BlockSpec((peers, SENT, READ_COLS), lambda g, p: (0, 0, g * steps + p)),
            pl.BlockSpec((ROWS, 2 * HEADS), lambda g, p: (0, 0)),
            pl.BlockSpec((8, READ_COLS), lambda g, p: (0, g * steps + p)),
        ],
        out_specs=[
            pl.BlockSpec((ROWS, READ_COLS), lambda g, p: (0, g * steps + p)),
            pl.BlockSpec((1, ROWS), lambda g, p: (0, 0)),
        ],
        scratch_shapes=[pltpu.VMEM((ROWS, 128), jnp.float32)],
        cost_estimate=pl.CostEstimate(
            flops=2 * ROWS * STATE * HALF, transcendentals=0, bytes_accessed=14 << 20
        ),
        name="read_states",
        interpret=INTERPRET,
    )(mixed, conv_out, conv_out, gained, states, factor, rows)


def prepare(tokens, labels, step_weight, step_bias, decay_rate):
    step_raw = jnp.dot(tokens, step_weight, preferred_element_type=jnp.float32).astype(jnp.bfloat16)
    step_size = jax.nn.softplus(step_raw.astype(jnp.float32) + step_bias[None, :])
    seg = labels[KCONV - 1 :]
    change = (-step_size * decay_rate[None, :]).reshape(BLOCKS, SPAN, HEADS)
    log_decay = jnp.cumsum(change, axis=1)
    last = log_decay[:, SPAN - 1]
    seg_blocks = seg.reshape(BLOCKS, SPAN)
    final = seg_blocks[:, SPAN - 1]
    before = jnp.concatenate([labels[KCONV - 2][None], final[:-1]])
    tail = jnp.where(
        (seg_blocks == final[:, None])[:, :, None], jnp.exp(last[:, None] - log_decay), 0.0
    ) * step_size.reshape(BLOCKS, SPAN, HEADS)
    factor = jnp.where((seg_blocks == before[:, None])[:, :, None], jnp.exp(log_decay), 0.0)
    passing = jnp.where((final == before)[:, None], jnp.exp(last), 0.0)
    masks = jnp.stack(
        [(labels[k : k + ROWS] == seg).astype(jnp.float32) for k in range(KCONV - 1)], axis=1
    )
    scaled = (log_decay * LOG2E).reshape(ROWS, HEADS).T
    sized = scaled - jnp.log2(step_size).T
    decay = jnp.concatenate(
        [
            scaled.reshape(HEADS // HEADS_STEP, HEADS_STEP, ROWS),
            sized.reshape(HEADS // HEADS_STEP, HEADS_STEP, ROWS),
        ],
        axis=1,
    )
    seg_rows = jnp.broadcast_to(seg.astype(jnp.float32)[None, :], (8, ROWS))
    return dict(
        tail=two_terms(tail.reshape(ROWS, HEADS)),
        factor=two_terms(factor.reshape(ROWS, HEADS)),
        passing=passing,
        masks=masks,
        decay=decay,
        seg=seg_rows,
    )


def over_columns(values):
    return jnp.repeat(values, HEAD_DIM, axis=-1)


def per_device(
    stream_tokens,
    xbc_weight,
    step_weight,
    conv_weight,
    conv_bias,
    step_bias,
    decay_rate,
    skip_gain,
    norm_gain,
    segment_ids,
    page_target,
):
    request_groups = lax.axis_size("chip") * CORES
    tok_rows = stream_tokens.shape[0]
    page_rows = tok_rows // request_groups
    seq_at, core = lax.axis_index("seq"), lax.axis_index("core")
    swap = [(0, 1), (1, 0)]
    peers = lax.axis_size("seq")
    onward = [(i, i + 1) for i in range(peers - 1)]

    targets = page_target[0]
    pages = scatter_pages(stream_tokens.reshape(request_groups, page_rows, D), targets)
    own = lax.all_to_all(pages, REQ, split_axis=0, concat_axis=0, tiled=True)
    own, own_ids = lax.optimization_barrier((own, segment_ids))
    other = lax.ppermute(own, "core", swap)
    other_ids = lax.ppermute(own_ids, "core", swap)

    def in_order(first, second):
        return [jnp.where(core == 0, first, second), jnp.where(core == 0, second, first)]

    tokens = [blocks.reshape(tok_rows, D) for blocks in in_order(own, other)]
    ids = in_order(own_ids, other_ids)
    halos = lax.ppermute(jnp.stack([rows[tok_rows - HALO :] for rows in tokens]), "seq", onward)

    weight = lax.all_gather(xbc_weight.T, ALL, axis=0, tiled=True)

    def columns(values):
        return jnp.concatenate(
            [
                lax.dynamic_slice_in_dim(values, core * HALF, HALF, axis=-1),
                lax.dynamic_slice_in_dim(values, INNER + core * BC, BC, axis=-1),
                lax.dynamic_slice_in_dim(values, INNER + CORES * BC + core * BC, BC, axis=-1),
            ],
            axis=-1,
        )

    def heads(values):
        return lax.dynamic_slice_in_dim(values, core * HEADS, HEADS, axis=-1)

    def labels(ids):
        padded = jnp.concatenate([jnp.full((KCONV - 1,), -1, jnp.int32), ids[0]])
        return lax.dynamic_slice_in_dim(padded, seq_at * tok_rows, tok_rows + KCONV - 1)

    taps, bias = columns(conv_weight), columns(conv_bias[None, :])
    step_half, step_shift, rate = heads(step_weight), heads(step_bias), heads(decay_rate)
    gain = lax.dynamic_slice_in_dim(norm_gain[None, :], core * HALF, HALF, axis=-1)
    ahead = (jnp.arange(peers) < seq_at).astype(jnp.float32)
    fixed_rows = jnp.concatenate(
        [
            over_columns(heads(skip_gain)[None, :]),
            jnp.zeros((1, HALF), jnp.float32),
            jnp.broadcast_to(ahead[:, None], (peers, HALF)),
        ],
        axis=0,
    )

    at_core = core.astype(jnp.int32)[None]
    ready, rows, conv_out, gained, every = [], [], [], [], []
    for q in range(CORES):
        ready.append(prepare(tokens[q], labels(ids[q]), step_half, step_shift, rate))
        rows.append(jnp.concatenate([over_columns(ready[q]["passing"]), fixed_rows], axis=0))
    weight, ready, rows, halos, taps, bias, gain = lax.optimization_barrier(
        (weight, ready, rows, [halos[q] for q in range(CORES)], taps, bias, gain)
    )
    for q in range(CORES):
        one = ready[q]
        conv_out.append(
            project_conv(
                at_core, halos[q], tokens[q], weight, taps, bias, one["masks"]
            )
        )
        after_first, local = block_states(conv_out[q], one["tail"], rows[q])
        gained.append(after_first)
        every.append(lax.all_gather(local, "seq"))

    returned = []
    for q in range(CORES):
        decay = ready[q]["decay"]
        if q > 0:
            returned[0], decay = lax.optimization_barrier((returned[0], decay))
        mixed = mix_blocks(conv_out[q], decay, ready[q]["seg"])
        combined, power = read_states(
            mixed, conv_out[q], gained[q], every[q], ready[q]["factor"], rows[q]
        )
        power = power + lax.ppermute(power, "core", swap)
        scale = lax.rsqrt(power[0] / INNER + 1e-05)
        returned.append(
            (combined.astype(jnp.float32) * scale[:, None] * gain).astype(jnp.bfloat16)
        )
    even, odd = [
        lax.all_to_all(
            rows_out.reshape(request_groups, page_rows, HALF),
            REQ,
            split_axis=0,
            concat_axis=0,
            tiled=True,
        )
        for rows_out in returned
    ]
    return join_pages(even, odd, targets).reshape(tok_rows, INNER)


def solution(mesh):
    chips = mesh.shape["req"] // CORES
    by_core = Mesh(
        mesh.devices.reshape(mesh.shape["seq"], chips, CORES), ("seq", "chip", "core")
    )
    in_specs = (
        P(ALL, None),
        P(None, ALL),
        P(),
        P(),
        P(),
        P(),
        P(),
        P(),
        P(),
        P(REQ, None),
        P(ALL, None),
    )
    return jax.shard_map(
        per_device, mesh=by_core, in_specs=in_specs, out_specs=P(ALL, None), check_vma=False
    )
```

```python
from functools import partial

import jax
import jax.numpy as jnp
from jax import lax
from jax.experimental import pallas as pl
from jax.experimental.pallas import tpu as pltpu
from jax.sharding import Mesh, PartitionSpec as P

HEAD_DIM = 64
STATE = 128
KCONV = 4
SPAN = 256
INNER = 4096
D = 2048
CORES = 2
HEADS = 32
GROUPS = 2
HALF = 2048
BC = GROUPS * STATE
OWN = HALF + 2 * BC

ALL = ("seq", "chip", "core")
REQ = ("chip", "core")


def move(index_ref, source_ref, out_ref, sems, *, places):
    copies = []
    for k, (source, target) in enumerate(places(index_ref)):
        copies.append(
            pltpu.make_async_copy(source_ref.at[source], out_ref.at[target], sems.at[k])
        )
    for copy in copies:
        copy.start()
    for copy in copies:
        copy.wait()


def scatter_pages(pages, targets):
    count = pages.shape[0]
    return pl.pallas_call(
        partial(move, places=lambda index: [(k, index[k]) for k in range(count)]),
        out_shape=jax.ShapeDtypeStruct(pages.shape, pages.dtype),
        in_specs=[pl.BlockSpec(memory_space=pltpu.SMEM), pl.BlockSpec(memory_space=pl.ANY)],
        out_specs=pl.BlockSpec(memory_space=pltpu.VMEM),
        scratch_shapes=[pltpu.SemaphoreType.DMA((count,))],
        name="scatter_pages",
    )(targets, pages)


def join_kernel(target_ref, pages_ref, *rest, which):
    out_ref, held_ref, read_sems, write_sems = rest[-4:]
    count = pages_ref.shape[0]

    def read(page, k, half):
        return pltpu.make_async_copy(
            pages_ref.at[page],
            held_ref.at[k, :, pl.ds(half * HALF, HALF)],
            read_sems.at[CORES * k + half],
        )

    def write(k):
        return pltpu.make_async_copy(held_ref.at[k], out_ref.at[k], write_sems.at[k])

    def for_mine(act):
        for k in range(count):
            pl.when(target_ref[k] % CORES == which)(partial(act, k))

    def start_reads(k):
        for half in range(CORES):
            read(target_ref[k] - which + half, k, half).start()

    def pass_on(k):
        for half in range(CORES):
            read(0, k, half).wait()
        write(k).start()

    def finish(k):
        write(k).wait()

    for_mine(start_reads)
    for_mine(pass_on)
    for_mine(finish)


def join_pages(which, pages, targets, behind=()):
    count, rows, width = pages.shape
    return pl.pallas_call(
        partial(join_kernel, which=which),
        out_shape=jax.ShapeDtypeStruct((count, rows, CORES * width), pages.dtype),
        in_specs=[pl.BlockSpec(memory_space=pltpu.SMEM)]
        + [pl.BlockSpec(memory_space=pl.ANY)] * (1 + len(behind)),
        out_specs=pl.BlockSpec(memory_space=pl.ANY),
        input_output_aliases={2: 0} if behind else {},
        scratch_shapes=[
            pltpu.VMEM((count, rows, CORES * width), pages.dtype),
            pltpu.SemaphoreType.DMA((CORES * count,)),
            pltpu.SemaphoreType.DMA((count,)),
        ],
        cost_estimate=pl.CostEstimate(flops=0, transcendentals=0, bytes_accessed=4 << 20),
        name="join_pages",
    )(targets, pages, *behind)


INTERPRET = False
LOG2E = 1.4426950408889634
ROWS = 512
BLOCKS = ROWS // SPAN
CONV_COLS = 512
CHUNK = 256
HALO = 16
TERMS = 3
SENT = STATE + 16
HEADS_STEP = 4
STEP_COLS = HEADS_STEP * HEAD_DIM
READ_COLS = 512
PER_GROUP = HEADS // GROUPS
GROUP_COLS = PER_GROUP * HEAD_DIM


def conv_kernel(
    core_ref, halo_ref, tok_ref, left_ref, right_ref, taps_ref, bias_ref, mask_ref, out_ref, raw_ref
):
    del core_ref
    masks = [mask_ref[:, k : k + 1] for k in range(KCONV - 1)]
    for part, weight_ref in enumerate((left_ref, right_ref)):
        dims = (((1,), (1,)), ((), ()))
        raw_ref[part, :HALO, :] = (
            lax.dot_general(
                halo_ref[...], weight_ref[...], dims, preferred_element_type=jnp.float32
            )
            .astype(jnp.bfloat16)
            .astype(jnp.float32)
        )
        raw_ref[part, HALO:, :] = (
            lax.dot_general(tok_ref[...], weight_ref[...], dims, preferred_element_type=jnp.float32)
            .astype(jnp.bfloat16)
            .astype(jnp.float32)
        )
    for part in range(CONV_COLS // CHUNK):
        cols = slice(part * CHUNK, (part + 1) * CHUNK)
        summed = bias_ref[:, cols] + taps_ref[KCONV - 1 : KCONV, cols] * raw_ref[part, HALO:, :]
        for k in range(KCONV - 1):
            start = HALO - (KCONV - 1) + k
            summed = (
                summed
                + (taps_ref[k : k + 1, cols] * raw_ref[part, start : start + ROWS, :]) * masks[k]
            )
        out_ref[:, cols] = (summed * (0.5 + 0.5 * jnp.tanh(0.5 * summed))).astype(jnp.bfloat16)


def project_conv(core, halo, tokens, weight, taps, bias, masks):
    x_steps = HALF // CONV_COLS

    def chunk(right):
        def at(n, core_ref):
            x_chunk = core_ref[0] * (HALF // CHUNK) + 2 * n + right
            bc_chunk = INNER // CHUNK + right * CORES * BC // CHUNK + core_ref[0]
            return jnp.where(n < x_steps, x_chunk, bc_chunk), 0

        return pl.BlockSpec((CHUNK, D), at)

    return pl.pallas_call(
        conv_kernel,
        grid_spec=pltpu.PrefetchScalarGridSpec(
            num_scalar_prefetch=1,
            grid=(OWN // CONV_COLS,),
            in_specs=[
                pl.BlockSpec((HALO, D), lambda n, core_ref: (0, 0)),
                pl.BlockSpec((ROWS, D), lambda n, core_ref: (0, 0)),
                chunk(0),
                chunk(1),
                pl.BlockSpec((KCONV, CONV_COLS), lambda n, core_ref: (0, n)),
                pl.BlockSpec((1, CONV_COLS), lambda n, core_ref: (0, n)),
                pl.BlockSpec((ROWS, KCONV - 1), lambda n, core_ref: (0, 0)),
            ],
            out_specs=pl.BlockSpec((ROWS, CONV_COLS), lambda n, core_ref: (0, n)),
            scratch_shapes=[pltpu.VMEM((CONV_COLS // CHUNK, HALO + ROWS, CHUNK), jnp.float32)],
        ),
        out_shape=jax.ShapeDtypeStruct((ROWS, OWN), jnp.bfloat16),
        cost_estimate=pl.CostEstimate(
            flops=2 * (ROWS + HALO) * D * OWN, transcendentals=ROWS * OWN, bytes_accessed=15 << 20
        ),
        name="project_conv",
        interpret=INTERPRET,
    )(core, halo, tokens, weight, weight, taps, bias, masks)


def spread_heads(terms, first_head, columns):
    head = lax.broadcasted_iota(jnp.int32, (2 * HEADS, columns), 0) % HEADS
    column = lax.broadcasted_iota(jnp.int32, (2 * HEADS, columns), 1)
    chosen = (head == first_head + column // HEAD_DIM).astype(jnp.bfloat16)
    return jnp.dot(terms, chosen, preferred_element_type=jnp.float32)


def two_terms(values):
    upper = lax.reduce_precision(values, 8, 7)
    return jnp.concatenate([upper, values - upper], axis=-1).astype(jnp.bfloat16)


def state_kernel(x_ref, b_ref, tail_ref, row_ref, gained_ref, local_ref):
    tail = spread_heads(tail_ref[...], pl.program_id(0) * PER_GROUP, GROUP_COLS)
    weighted = (x_ref[...].astype(jnp.float32) * tail).astype(jnp.bfloat16)
    gained = [
        lax.dot_general(
            b_ref[b * SPAN : (b + 1) * SPAN, :],
            weighted[b * SPAN : (b + 1) * SPAN],
            (((0,), (0,)), ((), ())),
            preferred_element_type=jnp.float32,
        )
        for b in range(BLOCKS)
    ]
    gained_ref[...] = gained[0]
    local_ref[:STATE, :] = (row_ref[1:2, :] * gained[0] + gained[1]).astype(jnp.bfloat16)
    left = row_ref[0:1, :] * row_ref[1:2, :]
    row = lax.broadcasted_iota(jnp.int32, (SENT - STATE, GROUP_COLS), 0)
    terms = jnp.zeros((SENT - STATE, GROUP_COLS), jnp.float32)
    for at in range(TERMS):
        term = left.astype(jnp.bfloat16).astype(jnp.float32)
        terms = jnp.where(row == at, term, terms)
        left = left - term
    local_ref[STATE:, :] = terms.astype(jnp.bfloat16)


def block_states(conv_out, tail, rows):
    return pl.pallas_call(
        state_kernel,
        grid=(GROUPS,),
        out_shape=[
            jax.ShapeDtypeStruct((STATE, HALF), jnp.float32),
            jax.ShapeDtypeStruct((SENT, HALF), jnp.bfloat16),
        ],
        in_specs=[
            pl.BlockSpec((ROWS, GROUP_COLS), lambda g: (0, g)),
            pl.BlockSpec((ROWS, STATE), lambda g: (0, HALF // STATE + g)),
            pl.BlockSpec((ROWS, 2 * HEADS), lambda g: (0, 0)),
            pl.BlockSpec((8, GROUP_COLS), lambda g: (0, g)),
        ],
        out_specs=[
            pl.BlockSpec((STATE, GROUP_COLS), lambda g: (0, g)),
            pl.BlockSpec((SENT, GROUP_COLS), lambda g: (0, g)),
        ],
        cost_estimate=pl.CostEstimate(
            flops=2 * ROWS * HALF * STATE, transcendentals=0, bytes_accessed=4 << 20
        ),
        name="block_states",
        interpret=INTERPRET,
    )(conv_out, conv_out, tail, rows)


def mixing_kernel(x_ref, b_ref, c_ref, decay_ref, seg_ref, out_ref, scores_ref, bias_ref):
    @pl.when(pl.program_id(1) == 0)
    def _():
        at = lax.broadcasted_iota(jnp.int32, (SPAN, SPAN), 0)
        source = lax.broadcasted_iota(jnp.int32, (SPAN, SPAN), 1)
        for b in range(BLOCKS):
            rows = slice(b * SPAN, (b + 1) * SPAN)
            scores_ref[b] = lax.dot_general(
                c_ref[rows, :],
                b_ref[rows, :],
                (((1,), (1,)), ((), ())),
                preferred_element_type=jnp.float32,
            )
            across = seg_ref[:, rows]
            down = across.T[:, 0:1]
            allowed = (down == across[0:1, :]) & (at >= source)
            bias_ref[b] = jnp.where(allowed, 0.0, -1e30)

    half = SPAN // 2
    lane = lax.broadcasted_iota(jnp.int32, (half, 2 * HEAD_DIM), 1)
    for b in range(BLOCKS):
        decay = decay_ref[0, :, b * SPAN : (b + 1) * SPAN]
        down = decay.T
        for pair in range(HEADS_STEP // 2):
            cols = slice(pair * 2 * HEAD_DIM, (pair + 1) * 2 * HEAD_DIM)
            for part in range(2):
                reach = (part + 1) * half
                rows = slice(part * half, reach)
                mixing = []
                for head in (2 * pair, 2 * pair + 1):
                    spread = (
                        down[rows, head : head + 1]
                        - decay[HEADS_STEP + head : HEADS_STEP + head + 1, :reach]
                    )
                    mixing.append(
                        (
                            jnp.exp2(spread + bias_ref[b, rows, :reach])
                            * scores_ref[b, rows, :reach]
                        ).astype(jnp.bfloat16)
                    )
                found = jnp.dot(
                    jnp.concatenate(mixing, axis=0),
                    x_ref[b * SPAN : b * SPAN + reach, cols],
                    preferred_element_type=jnp.float32,
                )
                out_ref[b * SPAN + part * half : b * SPAN + reach, cols] = jnp.where(
                    lane < HEAD_DIM, found[:half], found[half:]
                ).astype(jnp.bfloat16)


def mix_blocks(conv_out, decay, seg):
    steps = PER_GROUP // HEADS_STEP
    return pl.pallas_call(
        mixing_kernel,
        grid=(GROUPS, steps),
        out_shape=jax.ShapeDtypeStruct((ROWS, HALF), jnp.bfloat16),
        in_specs=[
            pl.BlockSpec((ROWS, STEP_COLS), lambda g, p: (0, g * steps + p)),
            pl.BlockSpec((ROWS, STATE), lambda g, p: (0, HALF // STATE + g)),
            pl.BlockSpec((ROWS, STATE), lambda g, p: (0, HALF // STATE + GROUPS + g)),
            pl.BlockSpec((1, 8, ROWS), lambda g, p: (g * steps + p, 0, 0)),
            pl.BlockSpec((8, ROWS), lambda g, p: (0, 0)),
        ],
        out_specs=pl.BlockSpec((ROWS, STEP_COLS), lambda g, p: (0, g * steps + p)),
        scratch_shapes=[pltpu.VMEM((BLOCKS, SPAN, SPAN), jnp.float32)] * 2,
        cost_estimate=pl.CostEstimate(
            flops=2 * ROWS * SPAN * HALF,
            transcendentals=ROWS * SPAN * HEADS,
            bytes_accessed=7 << 20,
        ),
        name="mix_blocks",
        interpret=INTERPRET,
    )(conv_out, conv_out, conv_out, decay, seg)


def readout_kernel(
    y_ref, x_ref, c_ref, gained_ref, states_ref, factor_ref, row_ref, out_ref, power_ref, part_ref
):
    steps = GROUP_COLS // READ_COLS
    at = pl.program_id(0) * steps + pl.program_id(1)
    incoming = jnp.zeros((STATE, READ_COLS), jnp.float32)
    for peer in range(states_ref.shape[0] - 1):
        terms = states_ref[peer, STATE:, :].astype(jnp.float32)
        through = (terms[0:1] + terms[1:2]) + terms[2:3]
        after = through * incoming + states_ref[peer, :STATE, :].astype(jnp.float32)
        incoming = jnp.where(row_ref[4 + peer : 5 + peer, :] > 0.5, after, incoming)
    second = row_ref[0:1, :] * incoming + gained_ref[...]
    factor = spread_heads(factor_ref[...], at * (READ_COLS // HEAD_DIM), READ_COLS)

    @pl.when(at == 0)
    def _():
        part_ref[...] = jnp.zeros_like(part_ref)

    for b, state in enumerate((incoming, second)):
        rows = slice(b * SPAN, (b + 1) * SPAN)
        readout = jnp.dot(
            c_ref[rows, :], state.astype(jnp.bfloat16), preferred_element_type=jnp.float32
        )
        combined = (
            y_ref[rows, :].astype(jnp.float32)
            + readout * factor[rows]
            + row_ref[2:3, :] * x_ref[rows, :].astype(jnp.float32)
        )
        out_ref[rows, :] = combined.astype(jnp.bfloat16)
        squared = combined * combined
        total = squared[:, :128]
        for tile in range(1, READ_COLS // 128):
            total = total + squared[:, tile * 128 : (tile + 1) * 128]
        part_ref[rows, :] += total

    @pl.when(at == GROUPS * steps - 1)
    def _():
        power_ref[...] = jnp.sum(part_ref[...].T, axis=0, keepdims=True)


def read_states(mixed, conv_out, gained, states, factor, rows):
    steps = GROUP_COLS // READ_COLS
    peers = states.shape[0]
    return pl.pallas_call(
        readout_kernel,
        grid=(GROUPS, steps),
        out_shape=[
            jax.ShapeDtypeStruct((ROWS, HALF), jnp.bfloat16),
            jax.ShapeDtypeStruct((1, ROWS), jnp.float32),
        ],
        in_specs=[
            pl.BlockSpec((ROWS, READ_COLS), lambda g, p: (0, g * steps + p)),
            pl.BlockSpec((ROWS, READ_COLS), lambda g, p: (0, g * steps + p)),
            pl.BlockSpec((ROWS, STATE), lambda g, p: (0, HALF // STATE + GROUPS + g)),
            pl.BlockSpec((STATE, READ_COLS), lambda g, p: (0, g * steps + p)),
            pl.BlockSpec((peers, SENT, READ_COLS), lambda g, p: (0, 0, g * steps + p)),
            pl.BlockSpec((ROWS, 2 * HEADS), lambda g, p: (0, 0)),
            pl.BlockSpec((8, READ_COLS), lambda g, p: (0, g * steps + p)),
        ],
        out_specs=[
            pl.BlockSpec((ROWS, READ_COLS), lambda g, p: (0, g * steps + p)),
            pl.BlockSpec((1, ROWS), lambda g, p: (0, 0)),
        ],
        scratch_shapes=[pltpu.VMEM((ROWS, 128), jnp.float32)],
        cost_estimate=pl.CostEstimate(
            flops=2 * ROWS * STATE * HALF, transcendentals=0, bytes_accessed=14 << 20
        ),
        name="read_states",
        interpret=INTERPRET,
    )(mixed, conv_out, conv_out, gained, states, factor, rows)


def prepare(tokens, labels, step_weight, step_bias, decay_rate):
    step_raw = jnp.dot(tokens, step_weight, preferred_element_type=jnp.float32).astype(jnp.bfloat16)
    step_size = jax.nn.softplus(step_raw.astype(jnp.float32) + step_bias[None, :])
    seg = labels[KCONV - 1 :]
    change = (-step_size * decay_rate[None, :]).reshape(BLOCKS, SPAN, HEADS)
    log_decay = jnp.cumsum(change, axis=1)
    last = log_decay[:, SPAN - 1]
    seg_blocks = seg.reshape(BLOCKS, SPAN)
    final = seg_blocks[:, SPAN - 1]
    before = jnp.concatenate([labels[KCONV - 2][None], final[:-1]])
    tail = jnp.where(
        (seg_blocks == final[:, None])[:, :, None], jnp.exp(last[:, None] - log_decay), 0.0
    ) * step_size.reshape(BLOCKS, SPAN, HEADS)
    factor = jnp.where((seg_blocks == before[:, None])[:, :, None], jnp.exp(log_decay), 0.0)
    passing = jnp.where((final == before)[:, None], jnp.exp(last), 0.0)
    masks = jnp.stack(
        [(labels[k : k + ROWS] == seg).astype(jnp.float32) for k in range(KCONV - 1)], axis=1
    )
    scaled = (log_decay * LOG2E).reshape(ROWS, HEADS).T
    sized = scaled - jnp.log2(step_size).T
    decay = jnp.concatenate(
        [
            scaled.reshape(HEADS // HEADS_STEP, HEADS_STEP, ROWS),
            sized.reshape(HEADS // HEADS_STEP, HEADS_STEP, ROWS),
        ],
        axis=1,
    )
    seg_rows = jnp.broadcast_to(seg.astype(jnp.float32)[None, :], (8, ROWS))
    return dict(
        tail=two_terms(tail.reshape(ROWS, HEADS)),
        factor=two_terms(factor.reshape(ROWS, HEADS)),
        passing=passing,
        masks=masks,
        decay=decay,
        seg=seg_rows,
    )


def over_columns(values):
    return jnp.repeat(values, HEAD_DIM, axis=-1)


def per_device(
    stream_tokens,
    xbc_weight,
    step_weight,
    conv_weight,
    conv_bias,
    step_bias,
    decay_rate,
    skip_gain,
    norm_gain,
    segment_ids,
    page_target,
):
    request_groups = lax.axis_size("chip") * CORES
    tok_rows = stream_tokens.shape[0]
    page_rows = tok_rows // request_groups
    seq_at, core = lax.axis_index("seq"), lax.axis_index("core")
    swap = [(0, 1), (1, 0)]
    peers = lax.axis_size("seq")
    onward = [(i, i + 1) for i in range(peers - 1)]

    targets = page_target[0]
    pages = scatter_pages(stream_tokens.reshape(request_groups, page_rows, D), targets)
    own = lax.all_to_all(pages, REQ, split_axis=0, concat_axis=0, tiled=True)
    own, own_ids = lax.optimization_barrier((own, segment_ids))
    other = lax.ppermute(own, "core", swap)
    other_ids = lax.ppermute(own_ids, "core", swap)

    def in_order(first, second):
        return [jnp.where(core == 0, first, second), jnp.where(core == 0, second, first)]

    tokens = [blocks.reshape(tok_rows, D) for blocks in in_order(own, other)]
    ids = in_order(own_ids, other_ids)
    halos = lax.ppermute(jnp.stack([rows[tok_rows - HALO :] for rows in tokens]), "seq", onward)

    weight = lax.all_gather(xbc_weight.T, ALL, axis=0, tiled=True)

    def columns(values):
        return jnp.concatenate(
            [
                lax.dynamic_slice_in_dim(values, core * HALF, HALF, axis=-1),
                lax.dynamic_slice_in_dim(values, INNER + core * BC, BC, axis=-1),
                lax.dynamic_slice_in_dim(values, INNER + CORES * BC + core * BC, BC, axis=-1),
            ],
            axis=-1,
        )

    def heads(values):
        return lax.dynamic_slice_in_dim(values, core * HEADS, HEADS, axis=-1)

    def labels(ids):
        padded = jnp.concatenate([jnp.full((KCONV - 1,), -1, jnp.int32), ids[0]])
        return lax.dynamic_slice_in_dim(padded, seq_at * tok_rows, tok_rows + KCONV - 1)

    taps, bias = columns(conv_weight), columns(conv_bias[None, :])
    step_half, step_shift, rate = heads(step_weight), heads(step_bias), heads(decay_rate)
    gain = lax.dynamic_slice_in_dim(norm_gain[None, :], core * HALF, HALF, axis=-1)
    ahead = (jnp.arange(peers) < seq_at).astype(jnp.float32)
    fixed_rows = jnp.concatenate(
        [
            over_columns(heads(skip_gain)[None, :]),
            jnp.zeros((1, HALF), jnp.float32),
            jnp.broadcast_to(ahead[:, None], (peers, HALF)),
        ],
        axis=0,
    )

    at_core = core.astype(jnp.int32)[None]
    ready, rows, conv_out, gained, every = [], [], [], [], []
    for q in range(CORES):
        ready.append(prepare(tokens[q], labels(ids[q]), step_half, step_shift, rate))
        rows.append(jnp.concatenate([over_columns(ready[q]["passing"]), fixed_rows], axis=0))
    weight, ready, rows, halos, taps, bias, gain = lax.optimization_barrier(
        (weight, ready, rows, [halos[q] for q in range(CORES)], taps, bias, gain)
    )
    for q in range(CORES):
        one = ready[q]
        conv_out.append(
            project_conv(
                at_core, halos[q], tokens[q], weight, taps, bias, one["masks"]
            )
        )
        after_first, local = block_states(conv_out[q], one["tail"], rows[q])
        gained.append(after_first)
        every.append(lax.all_gather(local, "seq"))

    returned = []
    for q in range(CORES):
        decay = ready[q]["decay"]
        if q > 0:
            returned[0], decay = lax.optimization_barrier((returned[0], decay))
        mixed = mix_blocks(conv_out[q], decay, ready[q]["seg"])
        combined, power = read_states(
            mixed, conv_out[q], gained[q], every[q], ready[q]["factor"], rows[q]
        )
        power = power + lax.ppermute(power, "core", swap)
        scale = lax.rsqrt(power[0] / INNER + 1e-05)
        returned.append(
            (combined.astype(jnp.float32) * scale[:, None] * gain).astype(jnp.bfloat16)
        )
    even, odd = [
        lax.all_to_all(
            rows_out.reshape(request_groups, page_rows, HALF),
            REQ,
            split_axis=0,
            concat_axis=0,
            tiled=True,
        )
        for rows_out in returned
    ]
    joined = join_pages(0, even, targets)
    return join_pages(1, odd, targets, (joined,)).reshape(tok_rows, INNER)


def solution(mesh):
    chips = mesh.shape["req"] // CORES
    by_core = Mesh(
        mesh.devices.reshape(mesh.shape["seq"], chips, CORES), ("seq", "chip", "core")
    )
    in_specs = (
        P(ALL, None),
        P(None, ALL),
        P(),
        P(),
        P(),
        P(),
        P(),
        P(),
        P(),
        P(REQ, None),
        P(ALL, None),
    )
    return jax.shard_map(
        per_device, mesh=by_core, in_specs=in_specs, out_specs=P(ALL, None), check_vma=False
    )
```
